32 devices in a mesh: dp: 16 (over z, x, core), tensor: 2 (over y).
Axes of the slice: x: 2, y: 2, z: 4, core: 2. Of those that a mesh axis runs over, the one named last changes fastest.
Arguments:
- tokens: bfloat16 [16, 1024, 2048], P('dp', 'tensor'), may hold values from -6 to 6
- lengths: int32 [16], P('dp'), may hold values from 256 to 1024, as said below
- gain: float32 [2048], replicated, may hold values from 0.1 to 1.9
- w_in: bfloat16 [2048, 2, 4096], P('dp', None, 'tensor'), may hold values from -0.125 to 0.125
- conv_weight: float32 [4, 4096], P(None, 'tensor'), may hold values from -3 to 3
- conv_bias: float32 [4096], P('tensor'), may hold values from -3 to 3
- w_x: bfloat16 [4096, 160], P('tensor'), may hold values from -0.09375 to 0.09375
- w_dt: bfloat16 [128, 4096], P(None, 'tensor'), may hold values from -0.5 to 0.5
- dt_bias: float32 [4096], P('tensor'), may hold values from -5.5 to -2
- a_log: float32 [16, 4096], P(None, 'tensor'), may hold values from -1 to 2.5
- d_skip: float32 [4096], P('tensor'), may hold values from 0.5 to 1.5
- w_out: bfloat16 [4096, 2048], P('tensor', 'dp'), may hold values from -0.1875 to 0.1875
- cotangent: bfloat16 [16, 1024, 2048], P('dp', 'tensor'), may hold values from -6 to 6
Outputs:
- mixed_out: bfloat16 [16, 1024, 2048], P('dp', 'tensor')
- d_tokens: float32 [16, 1024, 2048], P('dp', 'tensor')
- g_gain: float32 [2048], replicated
- g_w_in: float32 [2048, 2, 4096], P('dp', None, 'tensor')
- g_conv_weight: float32 [4, 4096], P(None, 'tensor')
- g_conv_bias: float32 [4096], P('tensor')
- g_w_x: float32 [4096, 160], P('tensor')
- g_w_dt: float32 [128, 4096], P(None, 'tensor')
- g_dt_bias: float32 [4096], P('tensor')
- g_a_log: float32 [16, 4096], P(None, 'tensor')
- g_d_skip: float32 [4096], P('tensor')
- g_w_out: float32 [4096, 2048], P('tensor', 'dp')
The draws below stay inside these ranges and needn't reach their ends.
Inputs may be any that keep to these rules, and one draw needn't show every extreme that they name: `lengths`: each sequence has at least 256 live slots, and one sequence has 1024; slots at or past a sequence's length are padding.
All inputs are finite; a program needn't handle non-finite values.
Results may differ from the reference program's by a relative error of at most 0.0096.
Values may be sent and summed in bfloat16 or wider, within the bound.
No kernel may reach another device: no remote copies, remote signals or barrier semaphores. Data moves between devices by JAX's collectives and lax.ppermute only.
A program may use at most 512 MiB of HBM per device.

```python
from functools import partial
import jax
import jax.numpy as jnp
from jax import lax

D = 2048
INNER = 4096
STATE = 16
RANK = 128
CONV = 4
SPAN = 256
LENGTH = 1024
SEQS = 16


def draw_lengths(key, part):
    first, second = jax.random.split(jax.random.fold_in(key, 17))
    values = jax.random.randint(first, (SEQS,), LENGTH // 4, LENGTH + 1)
    chosen = jax.random.randint(second, (), 0, SEQS)
    return jnp.where(jnp.arange(SEQS) == chosen, LENGTH, values).astype(jnp.int32)


def block_scale(stream_key, dims, shards, smallest, top_value):
    factor_of = 1.0
    for dim, shards_of in shards:
        draws = jax.random.uniform(jax.random.fold_in(jax.random.fold_in(stream_key, 6), dim), (shards_of,), jnp.float32, smallest / len(shards), top_value / len(shards))
        factor_of = factor_of * jnp.repeat(jnp.exp(draws), dims[dim] // shards_of).reshape((-1,) + (1,) * (len(dims) - 1 - dim))
    return factor_of


def normal_values(key, shape, scale, bound, cuts=(), held_as=jnp.bfloat16):
    level = block_scale(key, shape, cuts, -0.22, 0.18) if cuts else 1.0
    values = jax.random.normal(key, shape, jnp.float32) * scale * level
    return jnp.minimum(jnp.maximum(values, -bound), bound).astype(held_as)


def setup_inputs(seed: int = 0) -> dict:
    key_list = jax.random.split(jax.random.key(seed), 14)
    return {
        "tokens": normal_values(key_list[0], (SEQS, LENGTH, D), 1.0, 6.0, ((0, 16), (1, 2))),
        "lengths": draw_lengths(jax.random.fold_in(key_list[13], 71), 0),
        "gain": jnp.clip(1.0 + 0.18 * jax.random.normal(key_list[2], (D,), jnp.float32), 0.1, 1.9),
        "w_in": normal_values(key_list[3], (D, 2, INNER), D ** -0.5, 0.125, ((0, 16), (2, 2))),
        "conv_weight": normal_values(key_list[4], (CONV, INNER), CONV ** -0.5, 3.0, ((1, 2),), jnp.float32),
        "conv_bias": normal_values(key_list[5], (INNER,), 0.5, 3.0, ((0, 2),), jnp.float32),
        "w_x": normal_values(key_list[6], (INNER, RANK + 2 * STATE), INNER ** -0.5, 0.09375, ((0, 2),)),
        "w_dt": normal_values(key_list[7], (RANK, INNER), RANK ** -0.5, 0.5, ((1, 2),)),
        "dt_bias": jnp.clip(-5.5 + 3.5 * jax.random.uniform(key_list[8], (INNER,), jnp.float32) ** block_scale(key_list[8], (INNER,), ((0, 2),), -0.2, 0.2), -5.5, -2.0),
        "a_log": jnp.clip(-1.0 + 3.5 * jax.random.uniform(key_list[9], (STATE, INNER), jnp.float32) ** block_scale(key_list[9], (STATE, INNER), ((1, 2),), -0.2, 0.2), -1.0, 2.5),
        "d_skip": jnp.clip(0.5 + 1.0 * jax.random.uniform(key_list[10], (INNER,), jnp.float32) ** block_scale(key_list[10], (INNER,), ((0, 2),), -0.2, 0.2), 0.5, 1.5),
        "w_out": normal_values(key_list[11], (INNER, D), (INNER // 4) ** -0.5, 0.1875, ((0, 2), (1, 16))),
        "cotangent": normal_values(key_list[12], (SEQS, LENGTH, D), 1.0, 6.0, ((0, 16), (1, 2))),
    }


@jax.custom_vjp
def low(v):
    return lax.optimization_barrier(v.astype(jnp.bfloat16)).astype(jnp.float32)

@jax.custom_vjp
def low_back(v):
    return v

def low_keep(v):
    return (low(v), None)

def low_pass(kept, grad):
    return (grad,)

def back_keep(v):
    return (v, None)

def back_low(kept, grad):
    return (low(grad),)
low.defvjp(low_keep, low_pass)
low_back.defvjp(back_keep, back_low)
EPS = 1e-05
DT_LIMIT = 0.3
HIGHEST = lax.Precision.HIGHEST

def bounded_step(pre_sum, dt_bias):
    soft = jax.nn.softplus(pre_sum + dt_bias)
    return DT_LIMIT * soft / (DT_LIMIT + soft)

def convolve(inner_in, conv_weight, conv_bias):
    count = inner_in.shape[0]
    padded = jnp.pad(inner_in, ((CONV - 1, 0), (0, 0)))
    total = conv_bias + padded[0:count] * conv_weight[0]
    for offset in range(1, CONV):
        total = total + padded[offset:offset + count] * conv_weight[offset]
    return jax.nn.silu(total)

def scan_span(state, piece, decay):

    def advance(hidden, row):
        step_size, values, input_map, output_map = row
        hidden = jnp.exp(step_size[None, :] * decay) * hidden + input_map[:, None] * (step_size * values)[None, :]
        return (hidden, lax.optimization_barrier(jnp.sum(hidden * output_map[:, None], axis=0)))
    return lax.scan(advance, state, piece)

def one_sequence(params, sequence, length):
    gain, w_in, conv_weight, conv_bias, w_x, w_dt, dt_bias, a_log, d_skip, w_out = params
    scale = lax.rsqrt(lax.optimization_barrier(jnp.mean(sequence * sequence, axis=1, keepdims=True)) + EPS)
    normed = low(sequence * scale * gain)
    projected = low_back(jnp.einsum('ld,dkc->lkc', normed, w_in, precision=HIGHEST))
    convolved = low(convolve(projected[:, 0], conv_weight, conv_bias))
    coupled = low_back(jnp.dot(convolved, w_x, precision=HIGHEST))
    step_low = low(coupled[:, :RANK])
    pre_sum = low_back(jnp.dot(step_low, w_dt, precision=HIGHEST))
    step_size = bounded_step(pre_sum, dt_bias)
    decay = -jnp.exp(a_log)
    members = (step_size, convolved, coupled[:, RANK:RANK + STATE], coupled[:, RANK + STATE:])
    pieces = tuple((member.reshape((LENGTH // SPAN, SPAN) + member.shape[1:]) for member in members))
    initial = jnp.zeros((STATE, INNER), jnp.float32)
    _, scanned = lax.scan(jax.checkpoint(partial(scan_span, decay=decay)), initial, pieces)
    scanned = scanned.reshape(LENGTH, INNER)
    gated = low((scanned + d_skip * convolved) * jax.nn.silu(projected[:, 1]))
    branch = low_back(jnp.dot(gated, w_out, precision=HIGHEST))
    live = jnp.arange(LENGTH, dtype=jnp.int32) < length
    return sequence + jnp.where(live[:, None], branch, 0.0)

def reference(tokens, lengths, gain, w_in, conv_weight, conv_bias, w_x, w_dt, dt_bias, a_log, d_skip, w_out, cotangent):

    def forward(sequences, *params):

        def each(item):
            sequence, length = item
            return one_sequence(params, sequence, length)
        return lax.map(jax.checkpoint(each), (sequences, lengths))
    params = (gain, w_in.astype(jnp.float32), conv_weight, conv_bias, w_x.astype(jnp.float32), w_dt.astype(jnp.float32), dt_bias, a_log, d_skip, w_out.astype(jnp.float32))
    result, pull = jax.vjp(forward, tokens.astype(jnp.float32), *params)
    grads = pull(cotangent.astype(jnp.float32))
    return (result.astype(jnp.bfloat16), grads[0], grads[1], grads[2], grads[3], grads[4], grads[5], grads[6], grads[7], grads[8], grads[9], grads[10])
```

```python
import jax
import jax.numpy as jnp
from jax import lax
from jax.experimental import pallas as pl
from jax.experimental.pallas import tpu as pltpu
from jax.sharding import PartitionSpec as P


STATE = 16
RANK = 128
CONV = 4
EPS = 1e-05
LIM = 0.3
LOG2E = 1.4426950408889634
LANES = 128
SUB = 8
F32 = jnp.float32
BF = jnp.bfloat16


def work(seconds):
    return pl.CostEstimate(flops=int(seconds * 1e15), transcendentals=0, bytes_accessed=int(seconds * 1e12))


def after(value, *others):
    return lax.optimization_barrier((value,) + others)[0]


def put(ref, v):
    for g in range(ref.shape[0]):
        ref[g] = v[:, g*LANES:(g+1)*LANES]


def take(ref):
    return jnp.concatenate([ref[g] for g in range(ref.shape[0])], axis=1)


def spread_lanes(map_ref, lane_ref):
    high = map_ref[...].astype(BF).astype(F32)
    low = map_ref[...] - high
    spot = lax.broadcasted_iota(jnp.int32, (STATE, LANES), 1)
    ones = jnp.ones((2 * LANES, LANES), BF)

    def octet(i, _):
        base = i * SUB
        picked = [
            jnp.concatenate([jnp.where(spot == base + s, part, 0.0).astype(BF) for part in (high, low)], axis=1)
            for s in range(SUB)
        ]
        start = pl.multiple_of(base * STATE, SUB * STATE)
        lane_ref[pl.ds(start, SUB * STATE), :] = jnp.dot(
            jnp.concatenate(picked, axis=0), ones, preferred_element_type=F32
        )
        return 0

    lax.fori_loop(0, map_ref.shape[1] // SUB, octet, 0, unroll=8)


def rows_of(ref, row):
    return [ref[pl.ds(row + k * SUB, SUB), :] for k in range(2)]


def fold(ref, g):
    total = None
    for r in range(SUB):
        v = ref[g, pl.ds(r, SUB, stride=SUB), :]
        total = v if total is None else total + v
    return total


def fwd_kernel(low_ref, wdt_ref, bias_ref, x_ref, bt_ref, ct_ref, alog_ref, y_ref, dt_ref, slope_ref, hs_ref, last_ref, bl_ref, cl_ref,
               h_scr, dt_scr, dtx_scr, p_scr):
    span, width = x_ref.shape
    groups = width // LANES
    tc, cb = pl.program_id(0), pl.program_id(1)

    def sl(g):
        return pl.ds(g * LANES, LANES)

    pre = jnp.dot(low_ref[...], wdt_ref[...], preferred_element_type=F32) + bias_ref[...]
    tail = jnp.exp(-jnp.abs(pre))
    soft = jnp.maximum(pre, 0.0) + jnp.log1p(tail)
    share = LIM / (LIM + soft)
    dt = soft * share
    dt_ref[...] = dt
    slope_ref[...] = jnp.where(pre >= 0.0, 1.0, tail) / (1.0 + tail) * (share * share)
    put(dt_scr, dt)
    put(dtx_scr, dt * x_ref[...].astype(F32))

    @pl.when(tc == 0)
    def _():
        h_scr[cb] = jnp.zeros(h_scr.shape[1:], F32)

    @pl.when(cb == 0)
    def _():
        spread_lanes(bt_ref, bl_ref)
        spread_lanes(ct_ref, cl_ref)

    decay = -jnp.exp(alog_ref[...]) * LOG2E
    rate = [[decay[k * SUB : (k + 1) * SUB, g * LANES : (g + 1) * LANES] for k in range(2)] for g in range(groups)]

    def octet(i, h):
        h = [list(r) for r in h]
        base = pl.multiple_of(i * SUB, SUB)
        for s in range(SUB):
            t = base + s
            row = pl.multiple_of(t * STATE, STATE)
            b, c = rows_of(bl_ref, row), rows_of(cl_ref, row)
            for g in range(groups):
                dtb = dt_scr[g, pl.ds(t, SUB, stride=0), :]
                dxb = dtx_scr[g, pl.ds(t, SUB, stride=0), :]
                q = None
                for k in range(2):
                    hs_ref[pl.ds(row + k * SUB, SUB), sl(g)] = h[g][k]
                    h[g][k] = jnp.exp2(dtb * rate[g][k]) * h[g][k] + b[k] * dxb
                    p = h[g][k] * c[k]
                    q = p if q is None else q + p
                p_scr[g, pl.ds(s * SUB, SUB), :] = q
        for g in range(groups):
            y_ref[pl.ds(base, SUB), sl(g)] = fold(p_scr, g)
        return tuple(tuple(r) for r in h)

    h0 = tuple(tuple(h_scr[cb, pl.ds(k * SUB, SUB), sl(g)] for k in range(2)) for g in range(groups))
    hn = lax.fori_loop(0, span // SUB, octet, h0)
    for g in range(groups):
        for k in range(2):
            h_scr[cb, pl.ds(k * SUB, SUB), sl(g)] = hn[g][k]
            last_ref[pl.ds(k * SUB, SUB), sl(g)] = hn[g][k]


def scan_fwd(low, wdt, bias, x, bt, ct, alog, span=LANES, width=512):
    count, channels = x.shape
    width = min(width, channels)
    nt, nb, rank = count // span, channels // width, low.shape[1]
    groups = width // LANES
    tile = pl.BlockSpec((span, width), lambda t, c: (t, c))
    maps = pl.BlockSpec((STATE, span), lambda t, c: (0, t))
    lanes = pl.BlockSpec((span * STATE, LANES), lambda t, c: (t, 0))
    return pl.pallas_call(
        fwd_kernel,
        name="scan_fwd",
        grid=(nt, nb),
        in_specs=[
            pl.BlockSpec((span, rank), lambda t, c: (t, 0)),
            pl.BlockSpec((rank, width), lambda t, c: (0, c)),
            pl.BlockSpec((1, width), lambda t, c: (0, c)),
            tile,
            maps,
            maps,
            pl.BlockSpec((STATE, width), lambda t, c: (0, c)),
        ],
        out_specs=[
            tile,
            tile,
            tile,
            pl.BlockSpec((span * STATE, width), lambda t, c: (t, c)),
            pl.BlockSpec((STATE, width), lambda t, c: (0, c)),
            lanes,
            lanes,
        ],
        out_shape=[
            jax.ShapeDtypeStruct((count, channels), F32),
            jax.ShapeDtypeStruct((count, channels), F32),
            jax.ShapeDtypeStruct((count, channels), F32),
            jax.ShapeDtypeStruct((count * STATE, channels), F32),
            jax.ShapeDtypeStruct((STATE, channels), F32),
            jax.ShapeDtypeStruct((count * STATE, LANES), F32),
            jax.ShapeDtypeStruct((count * STATE, LANES), F32),
        ],
        scratch_shapes=[
            pltpu.VMEM((nb, STATE, width), F32),
            pltpu.VMEM((groups, span, LANES), F32),
            pltpu.VMEM((groups, span, LANES), F32),
            pltpu.VMEM((groups, SUB * SUB, LANES), F32),
        ],
        compiler_params=pltpu.CompilerParams(vmem_limit_bytes=48 << 20),
        cost_estimate=work(60e-6),
    )(low, wdt, bias.reshape(1, -1), x, bt, ct, alog)


def bwd_kernel(lowt_ref, wdt_ref, x_ref, dm_ref, dt_ref, slope_ref, hs_ref, last_ref, bl_ref, cl_ref, alog_ref, dskip_ref,
               dx_ref, dpart_ref, maps_ref, gwdt_ref, gal_ref, gvec_ref,
               g_scr, n_scr, dt_scr, dtx_scr, dm_scr, p1_scr, p2_scr, s1_scr, s2_scr, db_scr, dc_scr):
    span, width = x_ref.shape
    groups = width // LANES
    tc, cb = pl.program_id(0), pl.program_id(1)
    nb = pl.num_programs(1)

    def sl(g):
        return pl.ds(g * LANES, LANES)

    put(dt_scr, dt_ref[...])
    put(dtx_scr, dt_ref[...] * x_ref[...].astype(F32))
    put(dm_scr, dm_ref[...])

    @pl.when(tc == 0)
    def _():
        g_scr[cb] = jnp.zeros(g_scr.shape[1:], F32)
        n_scr[cb] = last_ref[...]
        gal_ref[cb] = jnp.zeros(gal_ref.shape[1:], F32)
        gvec_ref[cb] = jnp.zeros(gvec_ref.shape[1:], F32)
        gwdt_ref[cb] = jnp.zeros(gwdt_ref.shape[1:], F32)

    @pl.when(cb == 0)
    def _():
        db_scr[...] = jnp.zeros_like(db_scr)
        dc_scr[...] = jnp.zeros_like(dc_scr)
        dpart_ref[...] = jnp.zeros_like(dpart_ref)

    decay = -jnp.exp(alog_ref[...]) * LOG2E
    rate = [[decay[k * SUB : (k + 1) * SUB, g * LANES : (g + 1) * LANES] for k in range(2)] for g in range(groups)]

    def octet(j, carry):
        ag, ga, hn = [[list(r) for r in c] for c in carry]
        base = pl.multiple_of((span // SUB - 1 - j) * SUB, SUB)
        for s in reversed(range(SUB)):
            t = base + s
            row = pl.multiple_of(t * STATE, STATE)
            b, c = rows_of(bl_ref, row), rows_of(cl_ref, row)
            db = [db_scr[pl.ds(row + k * SUB, SUB), :] for k in range(2)]
            dc = [dc_scr[pl.ds(row + k * SUB, SUB), :] for k in range(2)]
            for g in range(groups):
                dtb = dt_scr[g, pl.ds(t, SUB, stride=0), :]
                dxb = dtx_scr[g, pl.ds(t, SUB, stride=0), :]
                dmb = dm_scr[g, pl.ds(t, SUB, stride=0), :]
                q1 = q2 = None
                for k in range(2):
                    hp = hs_ref[pl.ds(row + k * SUB, SUB), sl(g)]
                    da = dtb * rate[g][k]
                    adj = c[k] * dmb + ag[g][k]
                    dc[k] = dc[k] + dmb * hn[g][k]
                    db[k] = db[k] + adj * dxb
                    nag = jnp.exp2(da) * adj
                    q = (nag * hp) * da
                    ga[g][k] = ga[g][k] + q
                    gb = adj * b[k]
                    q1 = gb if q1 is None else q1 + gb
                    q2 = q if q2 is None else q2 + q
                    ag[g][k] = nag
                    hn[g][k] = hp
                p1_scr[g, pl.ds(s * SUB, SUB), :] = q1
                p2_scr[g, pl.ds(s * SUB, SUB), :] = q2
            for k in range(2):
                db_scr[pl.ds(row + k * SUB, SUB), :] = db[k]
                dc_scr[pl.ds(row + k * SUB, SUB), :] = dc[k]
        for g in range(groups):
            s1_scr[g, pl.ds(base, SUB), :] = fold(p1_scr, g)
            s2_scr[g, pl.ds(base, SUB), :] = fold(p2_scr, g)
        return tuple(tuple(tuple(r) for r in c) for c in (ag, ga, hn))

    def held(ref):
        return tuple(tuple(ref[cb, pl.ds(k * SUB, SUB), sl(g)] for k in range(2)) for g in range(groups))

    zero = jnp.zeros((SUB, LANES), F32)
    ga0 = tuple(tuple(zero for _ in range(2)) for _ in range(groups))
    ag, ga, hn = lax.fori_loop(0, span // SUB, octet, (held(g_scr), ga0, held(n_scr)))
    for g in range(groups):
        for k in range(2):
            g_scr[cb, pl.ds(k * SUB, SUB), sl(g)] = ag[g][k]
            n_scr[cb, pl.ds(k * SUB, SUB), sl(g)] = hn[g][k]
            gal_ref[cb, pl.ds(k * SUB, SUB), sl(g)] += ga[g][k] * (1.0 / LOG2E)
    dt = dt_ref[...]
    x = x_ref[...].astype(F32)
    dm = dm_ref[...]
    s1 = take(s1_scr)
    s2 = take(s2_scr) * (1.0 / LOG2E)
    dx_ref[...] = dm * dskip_ref[...] + dt * s1
    d_pre = (s2 / jnp.where(dt > 0.0, dt, 1.0) + x * s1) * slope_ref[...]
    gvec_ref[cb, 0:1, :] += jnp.sum(d_pre, axis=0, keepdims=True)
    gvec_ref[cb, 1:2, :] += jnp.sum(dm * x, axis=0, keepdims=True)
    dlow = d_pre.astype(BF)
    gwdt_ref[cb] += jnp.dot(lowt_ref[...], dlow, preferred_element_type=F32)
    dpart_ref[...] += lax.dot_general(dlow, wdt_ref[...], (((1,), (1,)), ((), ())), preferred_element_type=F32)

    @pl.when(cb == nb - 1)
    def _():
        ones = jnp.ones((SUB, LANES), BF)
        for n, ref in enumerate((db_scr, dc_scr)):
            total = lax.dot_general(ones, ref[...].astype(BF), (((1,), (1,)), ((), ())), preferred_element_type=F32)
            maps_ref[0, n : n + 1, :] = total[0:1]


def scan_bwd(low_t, wdt, x, dm, dt, slope, hs, last, bl, cl, alog, dskip, span=LANES, width=512):
    count, channels = x.shape
    width = min(width, channels)
    nt, nb, rank = count // span, channels // width, wdt.shape[0]
    groups = width // LANES
    tile = pl.BlockSpec((span, width), lambda t, c: (nt - 1 - t, c))
    lanes = pl.BlockSpec((span * STATE, LANES), lambda t, c: (nt - 1 - t, 0))
    return pl.pallas_call(
        bwd_kernel,
        name="scan_bwd",
        grid=(nt, nb),
        in_specs=[
            pl.BlockSpec((rank, span), lambda t, c: (0, nt - 1 - t)),
            pl.BlockSpec((rank, width), lambda t, c: (0, c)),
            tile,
            tile,
            tile,
            tile,
            pl.BlockSpec((span * STATE, width), lambda t, c: (nt - 1 - t, c)),
            pl.BlockSpec((STATE, width), lambda t, c: (0, c)),
            lanes,
            lanes,
            pl.BlockSpec((STATE, width), lambda t, c: (0, c)),
            pl.BlockSpec((1, width), lambda t, c: (0, c)),
        ],
        out_specs=[
            tile,
            pl.BlockSpec((span, rank), lambda t, c: (nt - 1 - t, 0)),
            pl.BlockSpec((1, 2, span * STATE), lambda t, c: (nt - 1 - t, 0, 0)),
            pl.BlockSpec((nb, rank, width), lambda t, c: (0, 0, 0)),
            pl.BlockSpec((nb, STATE, width), lambda t, c: (0, 0, 0)),
            pl.BlockSpec((nb, 2, width), lambda t, c: (0, 0, 0)),
        ],
        out_shape=[
            jax.ShapeDtypeStruct((count, channels), F32),
            jax.ShapeDtypeStruct((count, rank), F32),
            jax.ShapeDtypeStruct((nt, 2, span * STATE), F32),
            jax.ShapeDtypeStruct((nb, rank, width), F32),
            jax.ShapeDtypeStruct((nb, STATE, width), F32),
            jax.ShapeDtypeStruct((nb, 2, width), F32),
        ],
        scratch_shapes=[
            *[pltpu.VMEM((nb, STATE, width), F32)] * 2,
            *[pltpu.VMEM((groups, span, LANES), F32)] * 3,
            *[pltpu.VMEM((groups, SUB * SUB, LANES), F32)] * 2,
            *[pltpu.VMEM((groups, span, LANES), F32)] * 2,
            *[pltpu.VMEM((span * STATE, LANES), F32)] * 2,
        ],
        compiler_params=pltpu.CompilerParams(vmem_limit_bytes=48 << 20),
        cost_estimate=work(110e-6),
    )(low_t, wdt, x, dm, dt, slope, hs, last, bl, cl, alog, dskip.reshape(1, -1))


def conv_back_kernel(inner_ref, dx_ref, dcp_ref, dcpt_ref, wx_ref, cw_ref, cb_ref, din_ref, gsum_ref, gwx_ref, pad_ref, dpre_ref):
    L, W = inner_ref.shape
    rows = 256
    pad_ref[0:SUB, :] = jnp.zeros((SUB, W), F32)
    pad_ref[SUB:, :] = inner_ref[...]
    dpre_ref[L:, :] = jnp.zeros((SUB, W), F32)
    gwx_ref[...] = jnp.zeros_like(gwx_ref)
    sums = [jnp.zeros((1, W), F32)] * (CONV + 1)
    for r in range(0, L, rows):
        back = lax.dot_general(dcp_ref[r:r+rows, :], wx_ref[...], (((1,), (1,)), ((), ())), preferred_element_type=F32)
        taps = [pad_ref[r+SUB-(CONV-1)+j:r+SUB-(CONV-1)+j+rows, :] for j in range(CONV)]
        pre = cb_ref[...]
        for j in range(CONV):
            pre = pre + cw_ref[j:j+1, :] * taps[j]
        gate = jax.nn.sigmoid(pre)
        low = (pre * gate).astype(BF)
        d_pre = (dx_ref[r:r+rows, :] + back) * (gate * (1.0 + pre * (1.0 - gate)))
        dpre_ref[r:r+rows, :] = d_pre
        for j in range(CONV):
            sums[j] = sums[j] + jnp.sum(d_pre * taps[j], axis=0, keepdims=True)
        sums[CONV] = sums[CONV] + jnp.sum(d_pre, axis=0, keepdims=True)
        gwx_ref[...] += jnp.dot(dcpt_ref[:, r:r+rows], low, preferred_element_type=F32)
    for j in range(CONV + 1):
        gsum_ref[j:j+1, :] = sums[j]
    gsum_ref[CONV+1:, :] = jnp.zeros((SUB-CONV-1, W), F32)
    for r in range(0, L, rows):
        total = None
        for j in range(CONV):
            o = r + (CONV-1) - j
            v = cw_ref[j:j+1, :] * dpre_ref[o:o+rows, :]
            total = v if total is None else total + v
        din_ref[r:r+rows, :] = total.astype(BF)


def conv_back(inner, dx, dcp, wx, cw, cb, width=256):
    L, C = inner.shape; K = wx.shape[1]
    width = min(width, C)
    return pl.pallas_call(conv_back_kernel, name="conv_back", grid=(C//width,),
        in_specs=[pl.BlockSpec((L, width), lambda c: (0, c)),
                  pl.BlockSpec((L, width), lambda c: (0, c)),
                  pl.BlockSpec((L, K), lambda c: (0, 0)),
                  pl.BlockSpec((K, L), lambda c: (0, 0)),
                  pl.BlockSpec((width, K), lambda c: (c, 0)),
                  pl.BlockSpec((CONV, width), lambda c: (0, c)),
                  pl.BlockSpec((1, width), lambda c: (0, c))],
        out_specs=[pl.BlockSpec((L, width), lambda c: (0, c)),
                   pl.BlockSpec((SUB, width), lambda c: (0, c)),
                   pl.BlockSpec((K, width), lambda c: (0, c))],
        out_shape=[jax.ShapeDtypeStruct((L, C), BF), jax.ShapeDtypeStruct((SUB, C), F32), jax.ShapeDtypeStruct((K, C), F32)],
        scratch_shapes=[pltpu.VMEM((L+SUB, width), F32), pltpu.VMEM((L+SUB, width), F32)],
        compiler_params=pltpu.CompilerParams(vmem_limit_bytes=48<<20),
        cost_estimate=work(24e-6),
    )(inner, dx, dcp, dcp.T, wx, cw, cb.reshape(1, -1))


def swap(value):
    return lax.ppermute(value, "tensor", [(0, 1), (1, 0)])


def ordered(own, other):
    first = lax.axis_index("tensor") == 0
    return jnp.concatenate([jnp.where(first, own, other), jnp.where(first, other, own)], axis=0)


def gather_rows(own):
    if lax.axis_size("tensor") != 2:
        return lax.all_gather(own, "tensor", axis=0, tiled=True)
    return ordered(own, swap(own))


def total_tensor(part):
    if lax.axis_size("tensor") != 2:
        return lax.psum(part, "tensor")
    low = part.astype(BF)
    return low.astype(F32) + swap(low).astype(F32)


def scatter_product(left, product):
    count = lax.axis_size("tensor")
    if count != 2:
        return lax.psum_scatter(product(left), "tensor", scatter_dimension=0, tiled=True)
    half = left[0].shape[0] // 2
    index = lax.axis_index("tensor")

    def part(which):
        return product(tuple(lax.dynamic_slice_in_dim(v, which * half, half, 0) for v in left))

    sent = swap(part(1 - index).astype(BF))
    return part(index) + sent.astype(F32)


RING = (1, 3, 0, 2)
BEFORE = (2, 0, 3, 1)


def dp_spot():
    index = lax.axis_index("dp")
    return index // 4, (index // 2) % 2, index % 2


def over_core(v):
    return lax.ppermute(v, "dp", [(i, i ^ 1) for i in range(16)])


def over_x(v):
    return lax.ppermute(v, "dp", [(i, i ^ 2) for i in range(16)])


def over_ring(v):
    return lax.ppermute(v, "dp", [(i, RING[i // 4] * 4 + i % 4) for i in range(16)])


def over_z(v, shift):
    return lax.ppermute(v, "dp", [(i, (i + 4 * shift) % 16) for i in range(16)])


def part_of(v, which, count):
    size = v.shape[0] // count
    return lax.dynamic_slice_in_dim(v, which * size, size, 0)


def add_low(*terms):
    return sum(t.astype(F32) for t in terms).astype(BF)


def split_sum(quarter):
    z, x, c = dp_spot()
    first = quarter(1 - x, 1 - c)
    got = over_core(first)
    outer = add_low(quarter(1 - x, c), got)
    got = over_core(quarter(x, 1 - c))
    inner = add_low(quarter(x, c), got)
    order = [z]
    for _ in range(3):
        order.append(jnp.asarray(BEFORE, jnp.int32)[order[-1]])
    order = order[1:] + order[:1]
    crossed = [over_x(part_of(outer, place, 4)) for place in order]
    held = None
    for hop, place in enumerate(order):
        terms = [part_of(inner, place, 4), crossed[hop]]
        if held is not None:
            terms.append(held)
        if hop == 3:
            return sum(t.astype(F32) for t in terms)
        held = over_ring(add_low(*terms))


def total_dp(pack):
    if lax.axis_size("dp") != 16:
        return lax.psum(pack, "dp").astype(F32)
    _, x, c = dp_spot()
    half = add_low(part_of(pack, c, 2), over_core(part_of(pack, 1 - c, 2)))
    quarter = add_low(part_of(half, x, 2), over_x(part_of(half, 1 - x, 2)))
    whole = add_low(quarter, *(over_z(quarter, k) for k in (1, 2, 3)))
    half = paired(whole, over_x(whole), x)
    return paired(half, over_core(half), c).astype(F32)


def paired(own, other, place):
    first = place == 0
    return jnp.concatenate([jnp.where(first, own, other), jnp.where(first, other, own)], axis=0)


def total_all(row):
    if lax.axis_size("dp") != 16 or lax.axis_size("tensor") != 2:
        return lax.psum(row, ("dp", "tensor"))
    row = row + swap(row)
    row = row + over_core(row)
    row = row + over_x(row)
    return row + over_z(row, 1) + over_z(row, 2) + over_z(row, 3)


def convolve(inner_in, conv_weight, conv_bias):
    count = inner_in.shape[0]
    padded = jnp.pad(inner_in, ((CONV - 1, 0), (0, 0)))
    total = conv_bias + padded[0:count] * conv_weight[0]
    for offset in range(1, CONV):
        total = total + padded[offset : offset + count] * conv_weight[offset]
    return jax.nn.silu(total)


def mm(a, b):
    return jnp.dot(a, b, preferred_element_type=F32)


def mm_nt(a, b):
    return lax.dot_general(a, b, (((1,), (1,)), ((), ())), preferred_element_type=F32)


def mm_tn(a, b):
    return lax.dot_general(a, b, (((0,), (0,)), ((), ())), preferred_element_type=F32)


def body(
    tokens,
    lengths,
    gain,
    w_in,
    conv_weight,
    conv_bias,
    w_x,
    w_dt,
    dt_bias,
    a_log,
    d_skip,
    w_out,
    cotangent,
):
    rows_here = tokens.shape[1]
    width = conv_bias.shape[0]
    total_rows = rows_here * lax.axis_size("tensor")
    length = lengths[0]
    residual = tokens[0].astype(F32)
    scale = lax.rsqrt(jnp.mean(residual * residual, axis=1, keepdims=True) + EPS)
    normed = gather_rows((residual * scale * gain).astype(BF))
    cot_rows = gather_rows(after(cotangent[0], normed))
    w_inner = lax.all_gather(w_in[:, 0], "dp", axis=0, tiled=True)
    out_full = lax.all_gather(w_out, "dp", axis=1, tiled=True)
    w_gate = lax.all_gather(w_in[:, 1], "dp", axis=0, tiled=True)

    inner = mm(normed, w_inner)
    conv_low = convolve(inner, conv_weight, conv_bias).astype(BF)
    coupled = total_tensor(mm(conv_low, w_x))
    step_low = coupled[:, :RANK].astype(BF)
    input_map = coupled[:, RANK : RANK + STATE].T
    output_map = coupled[:, RANK + STATE :].T
    scanned, step_size, slope, states, last, input_lanes, output_lanes = scan_fwd(
        step_low, w_dt, dt_bias, conv_low, input_map, output_map, a_log
    )
    out_full, w_gate, scanned = lax.optimization_barrier((out_full, w_gate, scanned))

    live_all = jnp.arange(total_rows, dtype=jnp.int32) < length
    d_branch = jnp.where(live_all[:, None], cot_rows, jnp.zeros_like(cot_rows))
    d_gated = mm_nt(d_branch, out_full)
    gate_in = mm(normed, w_gate)
    sig = jax.nn.sigmoid(gate_in)
    opened = gate_in * sig
    mixed = scanned + d_skip * conv_low.astype(F32)
    gated = (mixed * opened).astype(BF)
    d_mixed = d_gated * opened
    d_gate = (d_gated * mixed * (sig * (1.0 + gate_in * (1.0 - sig)))).astype(BF)

    def spread(grad):
        return lax.psum_scatter(grad, "dp", scatter_dimension=0, tiled=True)

    part_out = mm_tn(d_branch, gated).astype(BF)
    part_gate = mm_tn(normed, d_gate).astype(BF)
    g_w_out = spread(part_out)
    g_w_gate = spread(part_gate)
    d_mixed = after(d_mixed, part_out, part_gate)
    branch = scatter_product((gated,), lambda v: mm(v[0], out_full))
    first_row = lax.axis_index("tensor") * rows_here
    live_here = first_row + jnp.arange(rows_here, dtype=jnp.int32) < length
    mixed_out = (residual + jnp.where(live_here[:, None], branch, 0.0)).astype(BF)

    d_scan, d_step_part, d_maps, g_w_dt, g_a_log, g_vec = scan_bwd(
        step_low.T,
        w_dt,
        conv_low,
        d_mixed,
        step_size,
        slope,
        states,
        last,
        input_lanes,
        output_lanes,
        a_log,
        d_skip,
    )
    d_maps = jnp.swapaxes(d_maps, 0, 1).reshape(2, total_rows, STATE)
    d_coupled = total_tensor(jnp.concatenate([d_step_part, d_maps[0], d_maps[1]], axis=1)).astype(BF)

    def joined(blocks):
        return jnp.swapaxes(blocks, 0, 1).reshape(blocks.shape[1], width)

    def gather_small(pieces):
        held = sum(p.shape[0] for p in pieces)
        padded = -(-held // 64) * 64
        pack = jnp.concatenate([p.astype(BF) for p in pieces] + [jnp.zeros((padded - held, width), BF)], axis=0)
        return total_dp(pack)

    early = gather_small([joined(g_w_dt), joined(g_a_log), joined(g_vec)])
    d_inner, g_conv, g_w_x = conv_back(inner, d_scan, d_coupled, w_x, conv_weight, conv_bias)
    late = gather_small([g_w_x, g_conv])

    if lax.axis_size("dp") == 16:
        own = w_in.shape[0]

        def quarter(x, c):
            at = x * (2 * own) + c * own
            columns = [lax.dynamic_slice_in_dim(normed, k * 4 * own + at, own, 1) for k in range(4)]
            return mm_tn(jnp.concatenate(columns, axis=1), d_inner).astype(BF)

        g_w_inner = split_sum(quarter)
    else:
        g_w_inner = spread(mm_tn(normed, d_inner).astype(BF))
    d_normed = scatter_product(
        (d_inner, d_gate), lambda v: mm_nt(v[0], w_inner) + mm_nt(v[1], w_gate)
    )
    g_gain = total_all(jnp.sum(residual * scale * d_normed, axis=0, keepdims=True))[0]
    weighted = d_normed * gain
    d_rows = (
        cotangent[0].astype(F32)
        + scale * weighted
        - residual * (scale * scale * scale) * jnp.mean(residual * weighted, axis=1, keepdims=True)
    )
    at = RANK + 2 * STATE
    g_w_x = late[:at].T
    g_conv_weight = late[at : at + CONV]
    g_conv_bias = late[at + CONV]
    g_w_dt = early[:RANK]
    g_a_log = early[RANK : RANK + STATE]
    g_dt_bias, g_d_skip = early[RANK + STATE], early[RANK + STATE + 1]
    g_w_gate, g_w_out = lax.optimization_barrier((g_w_gate, g_w_out, d_rows))[:2]
    g_w_in = jnp.stack([g_w_inner.astype(F32), g_w_gate.astype(F32)], axis=1)
    return (
        mixed_out[None],
        d_rows[None],
        g_gain,
        g_w_in,
        g_conv_weight,
        g_conv_bias,
        g_w_x,
        g_w_dt,
        g_dt_bias,
        g_a_log,
        g_d_skip,
        g_w_out.T.astype(F32),
    )


def solution(mesh):
    placed = (
        P("dp", "tensor", None),
        P("dp"),
        P(),
        P("dp", None, "tensor"),
        P(None, "tensor"),
        P("tensor"),
        P("tensor", None),
        P(None, "tensor"),
        P("tensor"),
        P(None, "tensor"),
        P("tensor"),
        P("tensor", "dp"),
        P("dp", "tensor", None),
    )
    return jax.shard_map(
        body,
        mesh=mesh,
        in_specs=placed,
        out_specs=(
            P("dp", "tensor", None),
            P("dp", "tensor", None),
            P(),
            P("dp", None, "tensor"),
            P(None, "tensor"),
            P("tensor"),
            P("tensor", None),
            P(None, "tensor"),
            P("tensor"),
            P(None, "tensor"),
            P("tensor"),
            P("tensor", "dp"),
        ),
        check_vma=False,
    )
```

```python
import jax
import jax.numpy as jnp
from jax import lax
from jax.experimental import pallas as pl
from jax.experimental.pallas import tpu as pltpu
from jax.sharding import PartitionSpec as P


STATE = 16
RANK = 128
CONV = 4
EPS = 1e-05
LIM = 0.3
LOG2E = 1.4426950408889634
LANES = 128
SUB = 8
F32 = jnp.float32
BF = jnp.bfloat16


def work(seconds):
    return pl.CostEstimate(flops=int(seconds * 1e15), transcendentals=0, bytes_accessed=int(seconds * 1e12))


def after(value, *others):
    return lax.optimization_barrier((value,) + others)[0]


def put(ref, v):
    for g in range(ref.shape[0]):
        ref[g] = v[:, g*LANES:(g+1)*LANES]


def take(ref):
    return jnp.concatenate([ref[g] for g in range(ref.shape[0])], axis=1)


def spread_lanes(map_ref, lane_ref):
    high = map_ref[...].astype(BF).astype(F32)
    low = map_ref[...] - high
    spot = lax.broadcasted_iota(jnp.int32, (STATE, LANES), 1)
    ones = jnp.ones((2 * LANES, LANES), BF)

    def octet(i, _):
        base = i * SUB
        picked = [
            jnp.concatenate([jnp.where(spot == base + s, part, 0.0).astype(BF) for part in (high, low)], axis=1)
            for s in range(SUB)
        ]
        start = pl.multiple_of(base * STATE, SUB * STATE)
        lane_ref[pl.ds(start, SUB * STATE), :] = jnp.dot(
            jnp.concatenate(picked, axis=0), ones, preferred_element_type=F32
        )
        return 0

    lax.fori_loop(0, map_ref.shape[1] // SUB, octet, 0, unroll=8)


def rows_of(ref, row):
    return [ref[pl.ds(row + k * SUB, SUB), :] for k in range(2)]


def fold(ref, g):
    total = None
    for r in range(SUB):
        v = ref[g, pl.ds(r, SUB, stride=SUB), :]
        total = v if total is None else total + v
    return total


def fwd_kernel(lowt_ref, wdt_ref, bias_ref, x_ref, bt_ref, ct_ref, alog_ref, y_ref, dt_ref, per_step_ref, per_sum_ref, hs_ref, last_ref, bl_ref, cl_ref,
               h_scr, dt_scr, dtx_scr, p_scr):
    span, width = x_ref.shape
    groups = width // LANES
    tc, cb = pl.program_id(0), pl.program_id(1)

    def sl(g):
        return pl.ds(g * LANES, LANES)

    pre = (
        lax.dot_general(lowt_ref[...], wdt_ref[...], (((0,), (0,)), ((), ())), preferred_element_type=F32)
        + bias_ref[...]
    )
    tail = jnp.exp(-jnp.abs(pre))
    soft = jnp.maximum(pre, 0.0) + jnp.log1p(tail)
    share = LIM / (LIM + soft)
    dt = soft * share
    dt_ref[...] = dt
    slope = jnp.where(pre >= 0.0, 1.0, tail) / (1.0 + tail) * (share * share)
    per_step_ref[...] = slope / jnp.where(dt > 0.0, dt, 1.0)
    per_sum_ref[...] = slope * x_ref[...].astype(F32)
    put(dt_scr, dt)
    put(dtx_scr, dt * x_ref[...].astype(F32))

    @pl.when(tc == 0)
    def _():
        h_scr[cb] = jnp.zeros(h_scr.shape[1:], F32)

    @pl.when(cb == 0)
    def _():
        spread_lanes(bt_ref, bl_ref)
        spread_lanes(ct_ref, cl_ref)

    decay = -jnp.exp(alog_ref[...]) * LOG2E
    rate = [[decay[k * SUB : (k + 1) * SUB, g * LANES : (g + 1) * LANES] for k in range(2)] for g in range(groups)]

    def octet(i, h):
        h = [list(r) for r in h]
        base = pl.multiple_of(i * SUB, SUB)
        for s in range(SUB):
            t = base + s
            row = pl.multiple_of(t * STATE, STATE)
            b, c = rows_of(bl_ref, row), rows_of(cl_ref, row)
            for g in range(groups):
                dtb = dt_scr[g, pl.ds(t, SUB, stride=0), :]
                dxb = dtx_scr[g, pl.ds(t, SUB, stride=0), :]
                q = None
                for k in range(2):
                    hs_ref[pl.ds(row + k * SUB, SUB), sl(g)] = h[g][k]
                    h[g][k] = jnp.exp2(dtb * rate[g][k]) * h[g][k] + b[k] * dxb
                    p = h[g][k] * c[k]
                    q = p if q is None else q + p
                p_scr[g, pl.ds(s * SUB, SUB), :] = q
        for g in range(groups):
            y_ref[pl.ds(base, SUB), sl(g)] = fold(p_scr, g)
        return tuple(tuple(r) for r in h)

    h0 = tuple(tuple(h_scr[cb, pl.ds(k * SUB, SUB), sl(g)] for k in range(2)) for g in range(groups))
    hn = lax.fori_loop(0, span // SUB, octet, h0)
    for g in range(groups):
        for k in range(2):
            h_scr[cb, pl.ds(k * SUB, SUB), sl(g)] = hn[g][k]
            last_ref[pl.ds(k * SUB, SUB), sl(g)] = hn[g][k]


def scan_fwd(low_t, wdt, bias, x, bt, ct, alog, span=LANES, width=1024):
    count, channels = x.shape
    width = min(width, channels)
    nt, nb, rank = count // span, channels // width, wdt.shape[0]
    groups = width // LANES
    tile = pl.BlockSpec((span, width), lambda t, c: (t, c))
    maps = pl.BlockSpec((STATE, span), lambda t, c: (0, t))
    lanes = pl.BlockSpec((span * STATE, LANES), lambda t, c: (t, 0))
    return pl.pallas_call(
        fwd_kernel,
        name="scan_fwd",
        grid=(nt, nb),
        in_specs=[
            pl.BlockSpec((rank, span), lambda t, c: (0, t)),
            pl.BlockSpec((rank, width), lambda t, c: (0, c)),
            pl.BlockSpec((1, width), lambda t, c: (0, c)),
            tile,
            maps,
            maps,
            pl.BlockSpec((STATE, width), lambda t, c: (0, c)),
        ],
        out_specs=[
            tile,
            tile,
            tile,
            tile,
            pl.BlockSpec((span * STATE, width), lambda t, c: (t, c)),
            pl.BlockSpec((STATE, width), lambda t, c: (0, c)),
            lanes,
            lanes,
        ],
        out_shape=[
            jax.ShapeDtypeStruct((count, channels), F32),
            jax.ShapeDtypeStruct((count, channels), F32),
            jax.ShapeDtypeStruct((count, channels), F32),
            jax.ShapeDtypeStruct((count, channels), F32),
            jax.ShapeDtypeStruct((count * STATE, channels), F32),
            jax.ShapeDtypeStruct((STATE, channels), F32),
            jax.ShapeDtypeStruct((count * STATE, LANES), F32),
            jax.ShapeDtypeStruct((count * STATE, LANES), F32),
        ],
        scratch_shapes=[
            pltpu.VMEM((nb, STATE, width), F32),
            pltpu.VMEM((groups, span, LANES), F32),
            pltpu.VMEM((groups, span, LANES), F32),
            pltpu.VMEM((groups, SUB * SUB, LANES), F32),
        ],
        compiler_params=pltpu.CompilerParams(vmem_limit_bytes=58 << 20),
        cost_estimate=work(60e-6),
    )(low_t, wdt, bias.reshape(1, -1), x, bt, ct, alog)


def bwd_kernel(lowt_ref, wdt_ref, x_ref, dm_ref, dt_ref, per_step_ref, per_sum_ref, hs_ref, last_ref, bl_ref, cl_ref, alog_ref, dskip_ref,
               dx_ref, dcp_ref, gwdt_ref, gal_ref, gvec_ref,
               part_scr, g_scr, n_scr, dt_scr, dtx_scr, dm_scr, p1_scr, p2_scr, s1_scr, s2_scr, db_scr, dc_scr):
    span, width = x_ref.shape
    groups = width // LANES
    tc, cb = pl.program_id(0), pl.program_id(1)
    nb = pl.num_programs(1)

    def sl(g):
        return pl.ds(g * LANES, LANES)

    put(dt_scr, dt_ref[...])
    put(dtx_scr, dt_ref[...] * x_ref[...].astype(F32))
    put(dm_scr, dm_ref[...])

    @pl.when(tc == 0)
    def _():
        g_scr[cb] = jnp.zeros(g_scr.shape[1:], F32)
        n_scr[cb] = last_ref[...]
        gal_ref[cb] = jnp.zeros(gal_ref.shape[1:], F32)
        gvec_ref[cb] = jnp.zeros(gvec_ref.shape[1:], F32)
        gwdt_ref[cb] = jnp.zeros(gwdt_ref.shape[1:], F32)

    @pl.when(cb == 0)
    def _():
        db_scr[...] = jnp.zeros_like(db_scr)
        dc_scr[...] = jnp.zeros_like(dc_scr)
        part_scr[...] = jnp.zeros_like(part_scr)

    decay = -jnp.exp(alog_ref[...]) * LOG2E
    rate = [[decay[k * SUB : (k + 1) * SUB, g * LANES : (g + 1) * LANES] for k in range(2)] for g in range(groups)]

    def octet(j, carry):
        ag, ga, hn = [[list(r) for r in c] for c in carry]
        base = pl.multiple_of((span // SUB - 1 - j) * SUB, SUB)
        for s in reversed(range(SUB)):
            t = base + s
            row = pl.multiple_of(t * STATE, STATE)
            b, c = rows_of(bl_ref, row), rows_of(cl_ref, row)
            db = [db_scr[pl.ds(row + k * SUB, SUB), :] for k in range(2)]
            dc = [dc_scr[pl.ds(row + k * SUB, SUB), :] for k in range(2)]
            for g in range(groups):
                dtb = dt_scr[g, pl.ds(t, SUB, stride=0), :]
                dxb = dtx_scr[g, pl.ds(t, SUB, stride=0), :]
                dmb = dm_scr[g, pl.ds(t, SUB, stride=0), :]
                q1 = q2 = None
                for k in range(2):
                    hp = hs_ref[pl.ds(row + k * SUB, SUB), sl(g)]
                    da = dtb * rate[g][k]
                    adj = c[k] * dmb + ag[g][k]
                    dc[k] = dc[k] + dmb * hn[g][k]
                    db[k] = db[k] + adj * dxb
                    nag = jnp.exp2(da) * adj
                    q = (nag * hp) * da
                    ga[g][k] = ga[g][k] + q
                    gb = adj * b[k]
                    q1 = gb if q1 is None else q1 + gb
                    q2 = q if q2 is None else q2 + q
                    ag[g][k] = nag
                    hn[g][k] = hp
                p1_scr[g, pl.ds(s * SUB, SUB), :] = q1
                p2_scr[g, pl.ds(s * SUB, SUB), :] = q2
            for k in range(2):
                db_scr[pl.ds(row + k * SUB, SUB), :] = db[k]
                dc_scr[pl.ds(row + k * SUB, SUB), :] = dc[k]
        for g in range(groups):
            s1_scr[g, pl.ds(base, SUB), :] = fold(p1_scr, g)
            s2_scr[g, pl.ds(base, SUB), :] = fold(p2_scr, g)
        return tuple(tuple(tuple(r) for r in c) for c in (ag, ga, hn))

    def held(ref):
        return tuple(tuple(ref[cb, pl.ds(k * SUB, SUB), sl(g)] for k in range(2)) for g in range(groups))

    zero = jnp.zeros((SUB, LANES), F32)
    ga0 = tuple(tuple(zero for _ in range(2)) for _ in range(groups))
    ag, ga, hn = lax.fori_loop(0, span // SUB, octet, (held(g_scr), ga0, held(n_scr)))
    for g in range(groups):
        for k in range(2):
            g_scr[cb, pl.ds(k * SUB, SUB), sl(g)] = ag[g][k]
            n_scr[cb, pl.ds(k * SUB, SUB), sl(g)] = hn[g][k]
            gal_ref[cb, pl.ds(k * SUB, SUB), sl(g)] += ga[g][k] * (1.0 / LOG2E)
    dt = dt_ref[...]
    x = x_ref[...].astype(F32)
    dm = dm_ref[...]
    s1 = take(s1_scr)
    s2 = take(s2_scr) * (1.0 / LOG2E)
    dx_ref[...] = dm * dskip_ref[...] + dt * s1
    d_pre = s2 * per_step_ref[...] + s1 * per_sum_ref[...]
    gvec_ref[cb, 0:1, :] += jnp.sum(d_pre, axis=0, keepdims=True)
    gvec_ref[cb, 1:2, :] += jnp.sum(dm * x, axis=0, keepdims=True)
    dlow = d_pre.astype(BF)
    gwdt_ref[cb] += jnp.dot(lowt_ref[...], dlow, preferred_element_type=F32)
    part_scr[...] += lax.dot_general(wdt_ref[...], dlow, (((1,), (1,)), ((), ())), preferred_element_type=F32)

    @pl.when(cb == nb - 1)
    def _():
        rank = part_scr.shape[0]
        dcp_ref[0:rank, :] = part_scr[...].astype(dcp_ref.dtype)
        ones = jnp.ones((STATE, LANES), BF)
        state = lax.broadcasted_iota(jnp.int32, (STATE, span * STATE), 0)
        spot = lax.broadcasted_iota(jnp.int32, (STATE, span * STATE), 1)
        row = lax.broadcasted_iota(jnp.int32, (span * STATE, span), 0)
        slot = lax.broadcasted_iota(jnp.int32, (span * STATE, span), 1)
        pick = jnp.where(row // STATE == slot, 1.0, 0.0).astype(BF)
        for n, ref in enumerate((db_scr, dc_scr)):
            total = lax.dot_general(ones, ref[...].astype(BF), (((1,), (1,)), ((), ())), preferred_element_type=F32)
            kept = jnp.where(spot % STATE == state, total, 0.0).astype(BF)
            at = rank + n * STATE
            dcp_ref[at : at + STATE, :] = jnp.dot(kept, pick, preferred_element_type=F32).astype(dcp_ref.dtype)


def scan_bwd(low_t, wdt, x, dm, dt, per_step, per_sum, hs, last, bl, cl, alog, dskip, span=LANES, width=1024):
    count, channels = x.shape
    width = min(width, channels)
    nt, nb, rank = count // span, channels // width, wdt.shape[0]
    groups = width // LANES
    tile = pl.BlockSpec((span, width), lambda t, c: (nt - 1 - t, c))
    lanes = pl.BlockSpec((span * STATE, LANES), lambda t, c: (nt - 1 - t, 0))
    return pl.pallas_call(
        bwd_kernel,
        name="scan_bwd",
        grid=(nt, nb),
        in_specs=[
            pl.BlockSpec((rank, span), lambda t, c: (0, nt - 1 - t)),
            pl.BlockSpec((rank, width), lambda t, c: (0, c)),
            tile,
            tile,
            tile,
            tile,
            tile,
            pl.BlockSpec((span * STATE, width), lambda t, c: (nt - 1 - t, c)),
            pl.BlockSpec((STATE, width), lambda t, c: (0, c)),
            lanes,
            lanes,
            pl.BlockSpec((STATE, width), lambda t, c: (0, c)),
            pl.BlockSpec((1, width), lambda t, c: (0, c)),
        ],
        out_specs=[
            tile,
            pl.BlockSpec((rank + 2 * STATE, span), lambda t, c: (0, nt - 1 - t)),
            pl.BlockSpec((nb, rank, width), lambda t, c: (0, 0, 0)),
            pl.BlockSpec((nb, STATE, width), lambda t, c: (0, 0, 0)),
            pl.BlockSpec((nb, 2, width), lambda t, c: (0, 0, 0)),
        ],
        out_shape=[
            jax.ShapeDtypeStruct((count, channels), F32),
            jax.ShapeDtypeStruct((rank + 2 * STATE, count), BF),
            jax.ShapeDtypeStruct((nb, rank, width), F32),
            jax.ShapeDtypeStruct((nb, STATE, width), F32),
            jax.ShapeDtypeStruct((nb, 2, width), F32),
        ],
        scratch_shapes=[
            pltpu.VMEM((rank, span), F32),
            *[pltpu.VMEM((nb, STATE, width), F32)] * 2,
            *[pltpu.VMEM((groups, span, LANES), F32)] * 3,
            *[pltpu.VMEM((groups, SUB * SUB, LANES), F32)] * 2,
            *[pltpu.VMEM((groups, span, LANES), F32)] * 2,
            *[pltpu.VMEM((span * STATE, LANES), F32)] * 2,
        ],
        compiler_params=pltpu.CompilerParams(vmem_limit_bytes=58 << 20),
        cost_estimate=work(110e-6),
    )(low_t, wdt, x, dm, dt, per_step, per_sum, hs, last, bl, cl, alog, dskip.reshape(1, -1))


def taps_at(pad_ref, g, row, rows):
    return [pad_ref[g, pl.ds(row + SUB - (CONV - 1) + j, rows), :] for j in range(CONV)]


def pre_of(taps, cw_ref, cb_ref, lanes):
    pre = cb_ref[:, lanes]
    for j in range(CONV):
        pre = pre + cw_ref[j : j + 1, lanes] * taps[j]
    return pre


def conv_kernel(inner_ref, wxt_ref, cw_ref, cb_ref, conv_ref, cpl_ref, pad_ref, sum_ref):
    count, width = inner_ref.shape
    rows = 128

    @pl.when(pl.program_id(0) == 0)
    def _():
        sum_ref[...] = jnp.zeros_like(sum_ref)

    for g in range(width // LANES):
        lanes = slice(g * LANES, (g + 1) * LANES)
        pad_ref[g, 0:SUB, :] = jnp.zeros((SUB, LANES), F32)
        pad_ref[g, SUB:, :] = inner_ref[:, lanes]

        def chunk(i, _, g=g, lanes=lanes):
            row = pl.multiple_of(i * rows, rows)
            pre = pre_of(taps_at(pad_ref, g, row, rows), cw_ref, cb_ref, lanes)
            conv_ref[pl.ds(row, rows), lanes] = (pre * jax.nn.sigmoid(pre)).astype(BF)
            return 0

        lax.fori_loop(0, count // rows, chunk, 0)
    sum_ref[...] += lax.dot_general(
        wxt_ref[...], conv_ref[...], (((1,), (1,)), ((), ())), preferred_element_type=F32
    )

    @pl.when(pl.program_id(0) == pl.num_programs(0) - 1)
    def _():
        cpl_ref[...] = sum_ref[...].astype(cpl_ref.dtype)


def conv_forward(inner, wxt, cw, cb, dtype, width=256):
    count, channels = inner.shape
    width = min(width, channels)
    cols = wxt.shape[0]
    return pl.pallas_call(
        conv_kernel,
        name="conv_forward",
        grid=(channels // width,),
        in_specs=[
            pl.BlockSpec((count, width), lambda c: (0, c)),
            pl.BlockSpec((cols, width), lambda c: (0, c)),
            pl.BlockSpec((CONV, width), lambda c: (0, c)),
            pl.BlockSpec((1, width), lambda c: (0, c)),
        ],
        out_specs=[
            pl.BlockSpec((count, width), lambda c: (0, c)),
            pl.BlockSpec((cols, count), lambda c: (0, 0)),
        ],
        out_shape=[
            jax.ShapeDtypeStruct((count, channels), BF),
            jax.ShapeDtypeStruct((cols, count), dtype),
        ],
        scratch_shapes=[pltpu.VMEM((width // LANES, count + SUB, LANES), F32), pltpu.VMEM((cols, count), F32)],
        compiler_params=pltpu.CompilerParams(vmem_limit_bytes=40 << 20),
        cost_estimate=work(12e-6),
    )(inner, wxt, cw, cb.reshape(1, -1))


def conv_back_kernel(inner_ref, dx_ref, dcp_ref, dcpt_ref, wxt_ref, cw_ref, cb_ref, din_ref, gsum_ref, gwx_ref,
                     pad_ref, dpre_ref, low_ref, back_ref):
    count, width = inner_ref.shape
    rows = 64
    back_ref[...] = jnp.dot(dcp_ref[...], wxt_ref[...], preferred_element_type=F32)
    gsum_ref[CONV + 1 :, :] = jnp.zeros((SUB - CONV - 1, width), F32)
    for g in range(width // LANES):
        lanes = slice(g * LANES, (g + 1) * LANES)
        pad_ref[g, 0:SUB, :] = jnp.zeros((SUB, LANES), F32)
        pad_ref[g, SUB:, :] = inner_ref[:, lanes]
        dpre_ref[g, count:, :] = jnp.zeros((SUB, LANES), F32)

        def chunk(i, sums, g=g, lanes=lanes):
            row = pl.multiple_of(i * rows, rows)
            taps = taps_at(pad_ref, g, row, rows)
            pre = pre_of(taps, cw_ref, cb_ref, lanes)
            gate = jax.nn.sigmoid(pre)
            conv = pre * gate
            low_ref[pl.ds(row, rows), lanes] = conv.astype(BF)
            d_pre = (dx_ref[pl.ds(row, rows), lanes] + back_ref[pl.ds(row, rows), lanes]) * (gate + conv - conv * gate)
            dpre_ref[g, pl.ds(row, rows), :] = d_pre
            new = [d_pre * t for t in taps] + [d_pre]
            return tuple(
                s + sum(n[k * SUB : (k + 1) * SUB] for k in range(rows // SUB)) for s, n in zip(sums, new)
            )

        zero = jnp.zeros((SUB, LANES), F32)
        sums = lax.fori_loop(0, count // rows, chunk, (zero,) * (CONV + 1))
        for j in range(CONV + 1):
            gsum_ref[j : j + 1, lanes] = jnp.sum(sums[j], axis=0, keepdims=True)

        def shift(i, _, g=g, lanes=lanes):
            row = pl.multiple_of(i * rows, rows)
            total = None
            for j in range(CONV):
                v = cw_ref[j : j + 1, lanes] * dpre_ref[g, pl.ds(row + CONV - 1 - j, rows), :]
                total = v if total is None else total + v
            din_ref[pl.ds(row, rows), lanes] = total.astype(BF)
            return 0

        lax.fori_loop(0, count // rows, shift, 0)
    gwx_ref[...] = jnp.dot(dcpt_ref[...], low_ref[...], preferred_element_type=F32)


def conv_back(inner, dx, dcpt, wxt, cw, cb, width=256):
    count, channels = inner.shape
    width = min(width, channels)
    cols = wxt.shape[0]
    return pl.pallas_call(
        conv_back_kernel,
        name="conv_back",
        grid=(channels // width,),
        in_specs=[
            pl.BlockSpec((count, width), lambda c: (0, c)),
            pl.BlockSpec((count, width), lambda c: (0, c)),
            pl.BlockSpec((count, cols), lambda c: (0, 0)),
            pl.BlockSpec((cols, count), lambda c: (0, 0)),
            pl.BlockSpec((cols, width), lambda c: (0, c)),
            pl.BlockSpec((CONV, width), lambda c: (0, c)),
            pl.BlockSpec((1, width), lambda c: (0, c)),
        ],
        out_specs=[
            pl.BlockSpec((count, width), lambda c: (0, c)),
            pl.BlockSpec((SUB, width), lambda c: (0, c)),
            pl.BlockSpec((cols, width), lambda c: (0, c)),
        ],
        out_shape=[
            jax.ShapeDtypeStruct((count, channels), BF),
            jax.ShapeDtypeStruct((SUB, channels), F32),
            jax.ShapeDtypeStruct((cols, channels), F32),
        ],
        scratch_shapes=[
            pltpu.VMEM((width // LANES, count + SUB, LANES), F32),
            pltpu.VMEM((width // LANES, count + SUB, LANES), F32),
            pltpu.VMEM((count, width), BF),
            pltpu.VMEM((count, width), F32),
        ],
        compiler_params=pltpu.CompilerParams(vmem_limit_bytes=40 << 20),
        cost_estimate=work(15e-6),
    )(inner, dx, dcpt.T, dcpt, wxt, cw, cb.reshape(1, -1))


def dual_kernel(which_ref, a_ref, b_ref, wa_ref, wb_ref, norm_ref, out_ref, sum_ref):
    del which_ref
    nt = (((1,), (1,)), ((), ()))
    out = lax.dot_general(a_ref[...], wa_ref[...], nt, preferred_element_type=F32)
    out = out + lax.dot_general(b_ref[...], wb_ref[...], nt, preferred_element_type=F32)
    out_ref[...] = out.astype(out_ref.dtype)
    sum_ref[...] = jnp.sum(norm_ref[...].astype(F32) * out, axis=0, keepdims=True)


def dual_product(which, rows, a, b, wa, wb, norm, dtype, tile=512):
    depth, count = a.shape[1], wa.shape[0]
    left = pl.BlockSpec((rows, depth), lambda n, w: (w[0], 0))
    right = pl.BlockSpec((tile, depth), lambda n, w: (n, 0))
    return pl.pallas_call(
        dual_kernel,
        name="dual_product",
        grid_spec=pltpu.PrefetchScalarGridSpec(
            num_scalar_prefetch=1,
            grid=(count // tile,),
            in_specs=[left, left, right, right, pl.BlockSpec((rows, tile), lambda n, w: (w[0], n))],
            out_specs=[
                pl.BlockSpec((rows, tile), lambda n, w: (0, n)),
                pl.BlockSpec((1, tile), lambda n, w: (0, n)),
            ],
        ),
        out_shape=[jax.ShapeDtypeStruct((rows, count), dtype), jax.ShapeDtypeStruct((1, count), F32)],
        compiler_params=pltpu.CompilerParams(vmem_limit_bytes=40 << 20),
        cost_estimate=work(15e-6),
    )(which.reshape(1).astype(jnp.int32), a, b, wa, wb, norm)


def swap(value):
    return lax.ppermute(value, "tensor", [(0, 1), (1, 0)])


def ordered(own, other):
    first = lax.axis_index("tensor") == 0
    return jnp.concatenate([jnp.where(first, own, other), jnp.where(first, other, own)], axis=0)


def gather_rows(own):
    if lax.axis_size("tensor") != 2:
        return lax.all_gather(own, "tensor", axis=0, tiled=True)
    return ordered(own, swap(own))


def total_tensor(part):
    if lax.axis_size("tensor") != 2:
        return lax.psum(part.astype(F32), "tensor")
    return part.astype(F32) + swap(part).astype(F32)


def dp_spot():
    index = lax.axis_index("dp")
    return index // 4, (index // 2) % 2, index % 2


def over_core(v):
    return lax.ppermute(v, "dp", [(i, i ^ 1) for i in range(16)])


def over_x(v):
    return lax.ppermute(v, "dp", [(i, i ^ 2) for i in range(16)])


def over_near(v):
    return lax.ppermute(v, "dp", [(i, i ^ 4) for i in range(16)])


def over_far(v):
    return lax.ppermute(v, "dp", [(i, i ^ 8) for i in range(16)])


def over_z(v, shift):
    return lax.ppermute(v, "dp", [(i, (i + 4 * shift) % 16) for i in range(16)])


def part_of(v, which, count):
    size = v.shape[0] // count
    return lax.dynamic_slice_in_dim(v, which * size, size, 0)


def pick(v, which, axis):
    return lax.dynamic_index_in_dim(v, which, axis, keepdims=False)


def add_low(*terms):
    return sum(t.astype(F32) for t in terms).astype(BF)


def paired(own, other, place):
    first = place == 0
    return jnp.concatenate([jnp.where(first, own, other), jnp.where(first, other, own)], axis=0)


def mm(a, b):
    return jnp.dot(a, b, preferred_element_type=F32)


def mm_nt(a, b):
    return lax.dot_general(a, b, (((1,), (1,)), ((), ())), preferred_element_type=F32)


def mm_tn(a, b):
    return lax.dot_general(a, b, (((0,), (0,)), ((), ())), preferred_element_type=F32)


def rows_out(residual, branch, length, first_row):
    live = first_row + jnp.arange(residual.shape[0], dtype=jnp.int32) < length
    return (residual + jnp.where(live[:, None], branch, 0.0)).astype(BF)


def rows_back(cotangent, residual, scale, gain, d_normed):
    weighted = d_normed * gain
    return (
        cotangent[0].astype(F32)
        + scale * weighted
        - residual * (scale * scale * scale) * jnp.mean(residual * weighted, axis=1, keepdims=True)
    )


def body(
    tokens,
    lengths,
    gain,
    w_in,
    conv_weight,
    conv_bias,
    w_x,
    w_dt,
    dt_bias,
    a_log,
    d_skip,
    w_out,
    cotangent,
):
    rows_here = tokens.shape[1]
    width = conv_bias.shape[0]
    total_rows = rows_here * lax.axis_size("tensor")
    paired_tensor = lax.axis_size("tensor") == 2
    grouped_dp = lax.axis_size("dp") == 16
    length = lengths[0]
    side = lax.axis_index("tensor")
    residual = tokens[0].astype(F32)
    scale = lax.rsqrt(jnp.mean(residual * residual, axis=1, keepdims=True) + EPS)
    normed = gather_rows((residual * scale * gain).astype(BF))
    cot_own = after(cotangent[0], normed)
    cot_other = swap(cot_own) if paired_tensor else lax.all_gather(cot_own, "tensor", axis=0, tiled=True)
    w_inner = lax.all_gather(w_in[:, 0], "dp", axis=0, tiled=True)
    w_gate = lax.all_gather(after(w_in, scale)[:, 1], "dp", axis=0, tiled=True)
    out_full = lax.all_gather(after(w_out, scale).T, "dp", axis=0, tiled=True)
    w_x_t = w_x.T

    inner = mm(normed, w_inner)
    conv_low, part = conv_forward(inner, w_x_t, conv_weight, conv_bias, BF)
    cot_own, cot_other, part_kept = lax.optimization_barrier((cot_own, cot_other, part))
    cot_rows = ordered(cot_own, cot_other) if paired_tensor else cot_other
    live_all = jnp.arange(total_rows, dtype=jnp.int32) < length
    d_branch = jnp.where(live_all[:, None], cot_rows, jnp.zeros_like(cot_rows))
    if paired_tensor:
        coupled = part_kept.astype(F32) + after(swap(part), d_branch).astype(F32)
    else:
        coupled = total_tensor(part)
    low_t = coupled[:RANK].astype(BF)
    scanned, step_size, per_step, per_sum, states, last, input_lanes, output_lanes = scan_fwd(
        low_t, w_dt, dt_bias, conv_low, coupled[RANK : RANK + STATE], coupled[RANK + STATE :], a_log
    )
    w_gate, scanned = lax.optimization_barrier((w_gate, scanned))
    gate_in = mm(normed, w_gate)
    sig = jax.nn.sigmoid(gate_in)
    opened = gate_in * sig
    mixed = scanned + d_skip * conv_low.astype(F32)
    gated = (mixed * opened).astype(BF)

    def spread(grad):
        return lax.psum_scatter(grad, "dp", scatter_dimension=0, tiled=True)

    part_out = mm_tn(d_branch, gated).astype(BF)
    g_w_out = spread(part_out)
    out_full = after(out_full, part_out)
    d_gated = mm(d_branch, out_full)
    d_mixed = d_gated * opened
    d_gate = (d_gated * mixed * (sig * (1.0 + gate_in * (1.0 - sig)))).astype(BF)
    part_gate = mm_tn(normed, d_gate).astype(BF)
    g_w_gate = spread(part_gate)

    def halves(v, which):
        return lax.dynamic_slice_in_dim(v, which * rows_here, rows_here, 0)

    d_mixed = after(d_mixed, part_gate)
    if not paired_tensor:
        branch = lax.psum_scatter(mm_nt(gated, out_full), "tensor", scatter_dimension=0, tiled=True)

    d_scan, d_part, g_w_dt, g_a_log, g_vec = scan_bwd(
        low_t,
        w_dt,
        conv_low,
        d_mixed,
        step_size,
        per_step,
        per_sum,
        states,
        last,
        input_lanes,
        output_lanes,
        a_log,
        d_skip,
    )

    def joined(blocks):
        return jnp.swapaxes(blocks, 0, 1).reshape(blocks.shape[1], width)

    def packed(pieces):
        held = sum(p.shape[0] for p in pieces)
        padded = -(-held // 64) * 64
        return jnp.concatenate([p.astype(BF) for p in pieces] + [jnp.zeros((padded - held, width), BF)], axis=0)

    if paired_tensor:
        branch_sent = mm_nt(after(halves(gated, 1 - side), d_part), out_full).astype(BF)
        d_coupled = (d_part.astype(F32) + after(swap(d_part), branch_sent).astype(F32)).astype(BF)
        branch_got = swap(after(branch_sent, d_coupled))
    else:
        d_coupled = total_tensor(d_part).astype(BF)
    d_inner, g_conv, g_w_x = conv_back(inner, d_scan, d_coupled, w_x_t, conv_weight, conv_bias)
    smalls = [joined(g_w_dt), joined(g_a_log), joined(g_vec), g_w_x, g_conv]
    if not grouped_dp or not paired_tensor:
        smalls = lax.psum(packed(smalls), "dp").astype(F32)
        g_w_inner = spread(mm_tn(normed, d_inner).astype(BF)).astype(F32)
        d_normed = lax.psum_scatter(
            mm_nt(d_inner, w_inner) + mm_nt(d_gate, w_gate), "tensor", scatter_dimension=0, tiled=True
        )
        g_gain = lax.psum(jnp.sum(residual * scale * d_normed, axis=0), ("dp", "tensor"))
        if paired_tensor:
            branch = mm_nt(halves(gated, side), out_full) + branch_got.astype(F32)
        d_rows = rows_back(cotangent, residual, scale, gain, d_normed)
        mixed_out = rows_out(residual, branch, length, side * rows_here)
    else:
        z, x, c = dp_spot()
        own, cut = w_in.shape[0], (7 * width) // 16

        pack = packed(smalls)
        core_got = over_core(part_of(pack, 1 - c, 2))
        part_b = mm_tn(after(normed, pack), d_inner[:, cut:]).astype(BF)
        half = add_low(part_of(pack, c, 2), after(core_got, part_b))
        x_got = over_x(part_of(half, 1 - x, 2))
        chips = after(part_b, half).reshape(8, 2, own, width - cut)
        chip_sent = pick(chips, 1 - c, 1)
        chip_got = over_core(chip_sent)
        part_a = mm_tn(after(normed, chip_sent), d_inner[:, :cut]).astype(BF)
        g_a = spread(part_a)
        quarter = add_low(part_of(half, x, 2), after(x_got, part_a))
        near_got = over_near(quarter)
        chip = add_low(pick(chips, c, 1), after(chip_got, quarter)).reshape(4, 2, own, width - cut)
        row_sent = pick(chip, 1 - x, 1)
        row_got = over_x(row_sent)
        sent, gain_sent = dual_product(
            1 - side, rows_here, after(d_inner, row_sent), d_gate, w_inner, w_gate, normed, BF
        )
        normed_got = swap(sent)
        pair = add_low(quarter, after(near_got, sent))
        far_got = over_far(pair)
        kept, gain_kept = dual_product(side, rows_here, after(d_inner, pair), d_gate, w_inner, w_gate, normed, F32)
        g_gain = gain_sent + gain_kept
        gain_got = over_core(g_gain)
        row = add_low(pick(chip, x, 1), after(row_got, kept))
        column_sent = [pick(row, (z + k) % 4, 0) for k in (1, 2, 3)]
        column_got = [over_z(column_sent[k - 1], k) for k in (1, 2, 3)]
        whole = add_low(pair, *lax.optimization_barrier((far_got,) + tuple(column_sent))[:1])
        x_got = over_x(whole)
        g_gain = g_gain + after(gain_got, whole)
        gain_got = over_x(g_gain)
        branch = mm_nt(after(halves(gated, side), g_gain), out_full) + branch_got.astype(F32)
        mixed_out = rows_out(residual, branch, length, side * rows_here)
        half = paired(whole, after(x_got, mixed_out), x)
        core_got = over_core(half)
        g_gain = g_gain + after(gain_got, mixed_out)
        gain_got = over_near(g_gain)
        smalls = paired(half, after(core_got, g_gain), c).astype(F32)
        g_gain = g_gain + after(gain_got, smalls)
        gain_got = over_far(g_gain)
        d_normed = kept + after(normed_got, g_gain).astype(F32)
        d_rows = rows_back(cotangent, residual, scale, gain, d_normed)
        g_gain = g_gain + after(gain_got, d_rows)
        gain_got = swap(g_gain)
        g_b = sum(
            (v.astype(F32) for v in lax.optimization_barrier(tuple(column_got) + (d_rows, g_gain))[:3]),
            pick(row, z, 0).astype(F32),
        )
        g_gain = (g_gain + after(gain_got, g_b))[0] / gain
        g_w_inner = jnp.concatenate([after(g_a, g_b).astype(F32), g_b], axis=1)

    g_w_dt = smalls[:RANK]
    at = RANK + STATE
    g_a_log = smalls[RANK:at]
    g_dt_bias, g_d_skip = smalls[at], smalls[at + 1]
    at += 2
    g_w_x = smalls[at : at + RANK + 2 * STATE].T
    at += RANK + 2 * STATE
    g_conv_weight = smalls[at : at + CONV]
    g_conv_bias = smalls[at + CONV]
    g_w_gate, g_w_out = lax.optimization_barrier((g_w_gate, g_w_out, d_rows))[:2]
    g_w_in = jnp.stack([g_w_inner, g_w_gate.astype(F32)], axis=1)
    return (
        mixed_out[None],
        d_rows[None],
        g_gain,
        g_w_in,
        g_conv_weight,
        g_conv_bias,
        g_w_x,
        g_w_dt,
        g_dt_bias,
        g_a_log,
        g_d_skip,
        g_w_out.T.astype(F32),
    )


def solution(mesh):
    placed = (
        P("dp", "tensor", None),
        P("dp"),
        P(),
        P("dp", None, "tensor"),
        P(None, "tensor"),
        P("tensor"),
        P("tensor", None),
        P(None, "tensor"),
        P("tensor"),
        P(None, "tensor"),
        P("tensor"),
        P("tensor", "dp"),
        P("dp", "tensor", None),
    )
    return jax.shard_map(
        body,
        mesh=mesh,
        in_specs=placed,
        out_specs=(
            P("dp", "tensor", None),
            P("dp", "tensor", None),
            P(),
            P("dp", None, "tensor"),
            P(None, "tensor"),
            P("tensor"),
            P("tensor", None),
            P(None, "tensor"),
            P("tensor"),
            P(None, "tensor"),
            P("tensor"),
            P("tensor", "dp"),
        ),
        check_vma=False,
    )
```

```python
import jax
import jax.numpy as jnp
from jax import lax
from jax.experimental import pallas as pl
from jax.experimental.pallas import tpu as pltpu
from jax.sharding import PartitionSpec as P


STATE = 16
RANK = 128
CONV = 4
EPS = 1e-05
LIM = 0.3
LOG2E = 1.4426950408889634
LANES = 128
SUB = 8
F32 = jnp.float32
BF = jnp.bfloat16


def work(seconds):
    return pl.CostEstimate(flops=int(seconds * 1e15), transcendentals=0, bytes_accessed=int(seconds * 1e12))


def after(value, *others):
    return lax.optimization_barrier((value,) + others)[0]


def put(ref, v):
    for g in range(ref.shape[0]):
        ref[g] = v[:, g*LANES:(g+1)*LANES]


def take(ref):
    return jnp.concatenate([ref[g] for g in range(ref.shape[0])], axis=1)


def spread_lanes(map_ref, lane_ref):
    high = map_ref[...].astype(BF).astype(F32)
    low = map_ref[...] - high
    spot = lax.broadcasted_iota(jnp.int32, (STATE, LANES), 1)
    ones = jnp.ones((2 * LANES, LANES), BF)

    def octet(i, _):
        base = i * SUB
        picked = [
            jnp.concatenate([jnp.where(spot == base + s, part, 0.0).astype(BF) for part in (high, low)], axis=1)
            for s in range(SUB)
        ]
        start = pl.multiple_of(base * STATE, SUB * STATE)
        lane_ref[pl.ds(start, SUB * STATE), :] = jnp.dot(
            jnp.concatenate(picked, axis=0), ones, preferred_element_type=F32
        )
        return 0

    lax.fori_loop(0, map_ref.shape[1] // SUB, octet, 0, unroll=8)


def rows_of(ref, row):
    return [ref[pl.ds(row + k * SUB, SUB), :] for k in range(2)]


def fold(ref, g):
    total = None
    for r in range(SUB):
        v = ref[g, pl.ds(r, SUB, stride=SUB), :]
        total = v if total is None else total + v
    return total


def fwd_kernel(lowt_ref, wdt_ref, bias_ref, x_ref, bt_ref, ct_ref, alog_ref, y_ref, dt_ref, slope_ref, hs_ref, last_ref, bl_ref, cl_ref,
               h_scr, dt_scr, dtx_scr, p_scr):
    span, width = x_ref.shape
    groups = width // LANES
    tc, cb = pl.program_id(0), pl.program_id(1)

    def sl(g):
        return pl.ds(g * LANES, LANES)

    pre = (
        lax.dot_general(lowt_ref[...], wdt_ref[...], (((0,), (0,)), ((), ())), preferred_element_type=F32)
        + bias_ref[...]
    )
    tail = jnp.exp(-jnp.abs(pre))
    soft = jnp.maximum(pre, 0.0) + jnp.log1p(tail)
    share = LIM / (LIM + soft)
    dt = soft * share
    dt_ref[...] = dt
    slope_ref[...] = jnp.where(pre >= 0.0, 1.0, tail) / (1.0 + tail) * (share * share)
    put(dt_scr, dt)
    put(dtx_scr, dt * x_ref[...].astype(F32))

    @pl.when(tc == 0)
    def _():
        h_scr[cb] = jnp.zeros(h_scr.shape[1:], F32)

    @pl.when(cb == 0)
    def _():
        spread_lanes(bt_ref, bl_ref)
        spread_lanes(ct_ref, cl_ref)

    decay = -jnp.exp(alog_ref[...]) * LOG2E
    rate = [[decay[k * SUB : (k + 1) * SUB, g * LANES : (g + 1) * LANES] for k in range(2)] for g in range(groups)]

    def octet(i, h):
        h = [list(r) for r in h]
        base = pl.multiple_of(i * SUB, SUB)
        for s in range(SUB):
            t = base + s
            row = pl.multiple_of(t * STATE, STATE)
            b, c = rows_of(bl_ref, row), rows_of(cl_ref, row)
            for g in range(groups):
                dtb = dt_scr[g, pl.ds(t, SUB, stride=0), :]
                dxb = dtx_scr[g, pl.ds(t, SUB, stride=0), :]
                q = None
                for k in range(2):
                    hs_ref[pl.ds(row + k * SUB, SUB), sl(g)] = h[g][k]
                    h[g][k] = jnp.exp2(dtb * rate[g][k]) * h[g][k] + b[k] * dxb
                    p = h[g][k] * c[k]
                    q = p if q is None else q + p
                p_scr[g, pl.ds(s * SUB, SUB), :] = q
        for g in range(groups):
            y_ref[pl.ds(base, SUB), sl(g)] = fold(p_scr, g)
        return tuple(tuple(r) for r in h)

    h0 = tuple(tuple(h_scr[cb, pl.ds(k * SUB, SUB), sl(g)] for k in range(2)) for g in range(groups))
    hn = lax.fori_loop(0, span // SUB, octet, h0)
    for g in range(groups):
        for k in range(2):
            h_scr[cb, pl.ds(k * SUB, SUB), sl(g)] = hn[g][k]
            last_ref[pl.ds(k * SUB, SUB), sl(g)] = hn[g][k]


def scan_fwd(low_t, wdt, bias, x, bt, ct, alog, span=LANES, width=512):
    count, channels = x.shape
    width = min(width, channels)
    nt, nb, rank = count // span, channels // width, wdt.shape[0]
    groups = width // LANES
    tile = pl.BlockSpec((span, width), lambda t, c: (t, c))
    maps = pl.BlockSpec((STATE, span), lambda t, c: (0, t))
    lanes = pl.BlockSpec((span * STATE, LANES), lambda t, c: (t, 0))
    return pl.pallas_call(
        fwd_kernel,
        name="scan_fwd",
        grid=(nt, nb),
        in_specs=[
            pl.BlockSpec((rank, span), lambda t, c: (0, t)),
            pl.BlockSpec((rank, width), lambda t, c: (0, c)),
            pl.BlockSpec((1, width), lambda t, c: (0, c)),
            tile,
            maps,
            maps,
            pl.BlockSpec((STATE, width), lambda t, c: (0, c)),
        ],
        out_specs=[
            tile,
            tile,
            tile,
            pl.BlockSpec((span * STATE, width), lambda t, c: (t, c)),
            pl.BlockSpec((STATE, width), lambda t, c: (0, c)),
            lanes,
            lanes,
        ],
        out_shape=[
            jax.ShapeDtypeStruct((count, channels), F32),
            jax.ShapeDtypeStruct((count, channels), F32),
            jax.ShapeDtypeStruct((count, channels), F32),
            jax.ShapeDtypeStruct((count * STATE, channels), F32),
            jax.ShapeDtypeStruct((STATE, channels), F32),
            jax.ShapeDtypeStruct((count * STATE, LANES), F32),
            jax.ShapeDtypeStruct((count * STATE, LANES), F32),
        ],
        scratch_shapes=[
            pltpu.VMEM((nb, STATE, width), F32),
            pltpu.VMEM((groups, span, LANES), F32),
            pltpu.VMEM((groups, span, LANES), F32),
            pltpu.VMEM((groups, SUB * SUB, LANES), F32),
        ],
        compiler_params=pltpu.CompilerParams(vmem_limit_bytes=48 << 20),
        cost_estimate=work(60e-6),
    )(low_t, wdt, bias.reshape(1, -1), x, bt, ct, alog)


def bwd_kernel(lowt_ref, wdt_ref, x_ref, dm_ref, dt_ref, slope_ref, hs_ref, last_ref, bl_ref, cl_ref, alog_ref, dskip_ref,
               dx_ref, dcp_ref, gwdt_ref, gal_ref, gvec_ref,
               part_scr, g_scr, n_scr, dt_scr, dtx_scr, dm_scr, p1_scr, p2_scr, s1_scr, s2_scr, db_scr, dc_scr):
    span, width = x_ref.shape
    groups = width // LANES
    tc, cb = pl.program_id(0), pl.program_id(1)
    nb = pl.num_programs(1)

    def sl(g):
        return pl.ds(g * LANES, LANES)

    put(dt_scr, dt_ref[...])
    put(dtx_scr, dt_ref[...] * x_ref[...].astype(F32))
    put(dm_scr, dm_ref[...])

    @pl.when(tc == 0)
    def _():
        g_scr[cb] = jnp.zeros(g_scr.shape[1:], F32)
        n_scr[cb] = last_ref[...]
        gal_ref[cb] = jnp.zeros(gal_ref.shape[1:], F32)
        gvec_ref[cb] = jnp.zeros(gvec_ref.shape[1:], F32)
        gwdt_ref[cb] = jnp.zeros(gwdt_ref.shape[1:], F32)

    @pl.when(cb == 0)
    def _():
        db_scr[...] = jnp.zeros_like(db_scr)
        dc_scr[...] = jnp.zeros_like(dc_scr)
        part_scr[...] = jnp.zeros_like(part_scr)

    decay = -jnp.exp(alog_ref[...]) * LOG2E
    rate = [[decay[k * SUB : (k + 1) * SUB, g * LANES : (g + 1) * LANES] for k in range(2)] for g in range(groups)]

    def octet(j, carry):
        ag, ga, hn = [[list(r) for r in c] for c in carry]
        base = pl.multiple_of((span // SUB - 1 - j) * SUB, SUB)
        for s in reversed(range(SUB)):
            t = base + s
            row = pl.multiple_of(t * STATE, STATE)
            b, c = rows_of(bl_ref, row), rows_of(cl_ref, row)
            db = [db_scr[pl.ds(row + k * SUB, SUB), :] for k in range(2)]
            dc = [dc_scr[pl.ds(row + k * SUB, SUB), :] for k in range(2)]
            for g in range(groups):
                dtb = dt_scr[g, pl.ds(t, SUB, stride=0), :]
                dxb = dtx_scr[g, pl.ds(t, SUB, stride=0), :]
                dmb = dm_scr[g, pl.ds(t, SUB, stride=0), :]
                q1 = q2 = None
                for k in range(2):
                    hp = hs_ref[pl.ds(row + k * SUB, SUB), sl(g)]
                    da = dtb * rate[g][k]
                    adj = c[k] * dmb + ag[g][k]
                    dc[k] = dc[k] + dmb * hn[g][k]
                    db[k] = db[k] + adj * dxb
                    nag = jnp.exp2(da) * adj
                    q = (nag * hp) * da
                    ga[g][k] = ga[g][k] + q
                    gb = adj * b[k]
                    q1 = gb if q1 is None else q1 + gb
                    q2 = q if q2 is None else q2 + q
                    ag[g][k] = nag
                    hn[g][k] = hp
                p1_scr[g, pl.ds(s * SUB, SUB), :] = q1
                p2_scr[g, pl.ds(s * SUB, SUB), :] = q2
            for k in range(2):
                db_scr[pl.ds(row + k * SUB, SUB), :] = db[k]
                dc_scr[pl.ds(row + k * SUB, SUB), :] = dc[k]
        for g in range(groups):
            s1_scr[g, pl.ds(base, SUB), :] = fold(p1_scr, g)
            s2_scr[g, pl.ds(base, SUB), :] = fold(p2_scr, g)
        return tuple(tuple(tuple(r) for r in c) for c in (ag, ga, hn))

    def held(ref):
        return tuple(tuple(ref[cb, pl.ds(k * SUB, SUB), sl(g)] for k in range(2)) for g in range(groups))

    zero = jnp.zeros((SUB, LANES), F32)
    ga0 = tuple(tuple(zero for _ in range(2)) for _ in range(groups))
    ag, ga, hn = lax.fori_loop(0, span // SUB, octet, (held(g_scr), ga0, held(n_scr)))
    for g in range(groups):
        for k in range(2):
            g_scr[cb, pl.ds(k * SUB, SUB), sl(g)] = ag[g][k]
            n_scr[cb, pl.ds(k * SUB, SUB), sl(g)] = hn[g][k]
            gal_ref[cb, pl.ds(k * SUB, SUB), sl(g)] += ga[g][k] * (1.0 / LOG2E)
    dt = dt_ref[...]
    x = x_ref[...].astype(F32)
    dm = dm_ref[...]
    s1 = take(s1_scr)
    s2 = take(s2_scr) * (1.0 / LOG2E)
    dx_ref[...] = dm * dskip_ref[...] + dt * s1
    d_pre = (s2 / jnp.where(dt > 0.0, dt, 1.0) + x * s1) * slope_ref[...]
    gvec_ref[cb, 0:1, :] += jnp.sum(d_pre, axis=0, keepdims=True)
    gvec_ref[cb, 1:2, :] += jnp.sum(dm * x, axis=0, keepdims=True)
    dlow = d_pre.astype(BF)
    gwdt_ref[cb] += jnp.dot(lowt_ref[...], dlow, preferred_element_type=F32)
    part_scr[...] += lax.dot_general(wdt_ref[...], dlow, (((1,), (1,)), ((), ())), preferred_element_type=F32)

    @pl.when(cb == nb - 1)
    def _():
        rank = part_scr.shape[0]
        dcp_ref[0:rank, :] = part_scr[...].astype(dcp_ref.dtype)
        ones = jnp.ones((STATE, LANES), BF)
        state = lax.broadcasted_iota(jnp.int32, (STATE, span * STATE), 0)
        spot = lax.broadcasted_iota(jnp.int32, (STATE, span * STATE), 1)
        row = lax.broadcasted_iota(jnp.int32, (span * STATE, span), 0)
        slot = lax.broadcasted_iota(jnp.int32, (span * STATE, span), 1)
        pick = jnp.where(row // STATE == slot, 1.0, 0.0).astype(BF)
        for n, ref in enumerate((db_scr, dc_scr)):
            total = lax.dot_general(ones, ref[...].astype(BF), (((1,), (1,)), ((), ())), preferred_element_type=F32)
            kept = jnp.where(spot % STATE == state, total, 0.0).astype(BF)
            at = rank + n * STATE
            dcp_ref[at : at + STATE, :] = jnp.dot(kept, pick, preferred_element_type=F32).astype(dcp_ref.dtype)


def scan_bwd(low_t, wdt, x, dm, dt, slope, hs, last, bl, cl, alog, dskip, span=LANES, width=512):
    count, channels = x.shape
    width = min(width, channels)
    nt, nb, rank = count // span, channels // width, wdt.shape[0]
    groups = width // LANES
    tile = pl.BlockSpec((span, width), lambda t, c: (nt - 1 - t, c))
    lanes = pl.BlockSpec((span * STATE, LANES), lambda t, c: (nt - 1 - t, 0))
    return pl.pallas_call(
        bwd_kernel,
        name="scan_bwd",
        grid=(nt, nb),
        in_specs=[
            pl.BlockSpec((rank, span), lambda t, c: (0, nt - 1 - t)),
            pl.BlockSpec((rank, width), lambda t, c: (0, c)),
            tile,
            tile,
            tile,
            tile,
            pl.BlockSpec((span * STATE, width), lambda t, c: (nt - 1 - t, c)),
            pl.BlockSpec((STATE, width), lambda t, c: (0, c)),
            lanes,
            lanes,
            pl.BlockSpec((STATE, width), lambda t, c: (0, c)),
            pl.BlockSpec((1, width), lambda t, c: (0, c)),
        ],
        out_specs=[
            tile,
            pl.BlockSpec((rank + 2 * STATE, span), lambda t, c: (0, nt - 1 - t)),
            pl.BlockSpec((nb, rank, width), lambda t, c: (0, 0, 0)),
            pl.BlockSpec((nb, STATE, width), lambda t, c: (0, 0, 0)),
            pl.BlockSpec((nb, 2, width), lambda t, c: (0, 0, 0)),
        ],
        out_shape=[
            jax.ShapeDtypeStruct((count, channels), F32),
            jax.ShapeDtypeStruct((rank + 2 * STATE, count), BF),
            jax.ShapeDtypeStruct((nb, rank, width), F32),
            jax.ShapeDtypeStruct((nb, STATE, width), F32),
            jax.ShapeDtypeStruct((nb, 2, width), F32),
        ],
        scratch_shapes=[
            pltpu.VMEM((rank, span), F32),
            *[pltpu.VMEM((nb, STATE, width), F32)] * 2,
            *[pltpu.VMEM((groups, span, LANES), F32)] * 3,
            *[pltpu.VMEM((groups, SUB * SUB, LANES), F32)] * 2,
            *[pltpu.VMEM((groups, span, LANES), F32)] * 2,
            *[pltpu.VMEM((span * STATE, LANES), F32)] * 2,
        ],
        compiler_params=pltpu.CompilerParams(vmem_limit_bytes=48 << 20),
        cost_estimate=work(110e-6),
    )(low_t, wdt, x, dm, dt, slope, hs, last, bl, cl, alog, dskip.reshape(1, -1))


def taps_at(pad_ref, g, row, rows):
    return [pad_ref[g, pl.ds(row + SUB - (CONV - 1) + j, rows), :] for j in range(CONV)]


def pre_of(taps, cw_ref, cb_ref, lanes):
    pre = cb_ref[:, lanes]
    for j in range(CONV):
        pre = pre + cw_ref[j : j + 1, lanes] * taps[j]
    return pre


def conv_kernel(inner_ref, wxt_ref, cw_ref, cb_ref, conv_ref, cpl_ref, pad_ref, sum_ref):
    count, width = inner_ref.shape
    rows = 128

    @pl.when(pl.program_id(0) == 0)
    def _():
        sum_ref[...] = jnp.zeros_like(sum_ref)

    for g in range(width // LANES):
        lanes = slice(g * LANES, (g + 1) * LANES)
        pad_ref[g, 0:SUB, :] = jnp.zeros((SUB, LANES), F32)
        pad_ref[g, SUB:, :] = inner_ref[:, lanes]

        def chunk(i, _, g=g, lanes=lanes):
            row = pl.multiple_of(i * rows, rows)
            pre = pre_of(taps_at(pad_ref, g, row, rows), cw_ref, cb_ref, lanes)
            conv_ref[pl.ds(row, rows), lanes] = (pre * jax.nn.sigmoid(pre)).astype(BF)
            return 0

        lax.fori_loop(0, count // rows, chunk, 0)
    sum_ref[...] += lax.dot_general(
        wxt_ref[...], conv_ref[...], (((1,), (1,)), ((), ())), preferred_element_type=F32
    )

    @pl.when(pl.program_id(0) == pl.num_programs(0) - 1)
    def _():
        cpl_ref[...] = sum_ref[...].astype(cpl_ref.dtype)


def conv_forward(inner, wxt, cw, cb, dtype, width=256):
    count, channels = inner.shape
    width = min(width, channels)
    cols = wxt.shape[0]
    return pl.pallas_call(
        conv_kernel,
        name="conv_forward",
        grid=(channels // width,),
        in_specs=[
            pl.BlockSpec((count, width), lambda c: (0, c)),
            pl.BlockSpec((cols, width), lambda c: (0, c)),
            pl.BlockSpec((CONV, width), lambda c: (0, c)),
            pl.BlockSpec((1, width), lambda c: (0, c)),
        ],
        out_specs=[
            pl.BlockSpec((count, width), lambda c: (0, c)),
            pl.BlockSpec((cols, count), lambda c: (0, 0)),
        ],
        out_shape=[
            jax.ShapeDtypeStruct((count, channels), BF),
            jax.ShapeDtypeStruct((cols, count), dtype),
        ],
        scratch_shapes=[pltpu.VMEM((width // LANES, count + SUB, LANES), F32), pltpu.VMEM((cols, count), F32)],
        compiler_params=pltpu.CompilerParams(vmem_limit_bytes=40 << 20),
        cost_estimate=work(12e-6),
    )(inner, wxt, cw, cb.reshape(1, -1))


def conv_back_kernel(inner_ref, dx_ref, dcp_ref, dcpt_ref, wxt_ref, cw_ref, cb_ref, din_ref, gsum_ref, gwx_ref,
                     pad_ref, dpre_ref, low_ref, back_ref):
    count, width = inner_ref.shape
    rows = 64
    back_ref[...] = jnp.dot(dcp_ref[...], wxt_ref[...], preferred_element_type=F32)
    gsum_ref[CONV + 1 :, :] = jnp.zeros((SUB - CONV - 1, width), F32)
    for g in range(width // LANES):
        lanes = slice(g * LANES, (g + 1) * LANES)
        pad_ref[g, 0:SUB, :] = jnp.zeros((SUB, LANES), F32)
        pad_ref[g, SUB:, :] = inner_ref[:, lanes]
        dpre_ref[g, count:, :] = jnp.zeros((SUB, LANES), F32)

        def chunk(i, sums, g=g, lanes=lanes):
            row = pl.multiple_of(i * rows, rows)
            taps = taps_at(pad_ref, g, row, rows)
            pre = pre_of(taps, cw_ref, cb_ref, lanes)
            gate = jax.nn.sigmoid(pre)
            conv = pre * gate
            low_ref[pl.ds(row, rows), lanes] = conv.astype(BF)
            d_pre = (dx_ref[pl.ds(row, rows), lanes] + back_ref[pl.ds(row, rows), lanes]) * (gate + conv - conv * gate)
            dpre_ref[g, pl.ds(row, rows), :] = d_pre
            new = [d_pre * t for t in taps] + [d_pre]
            return tuple(
                s + sum(n[k * SUB : (k + 1) * SUB] for k in range(rows // SUB)) for s, n in zip(sums, new)
            )

        zero = jnp.zeros((SUB, LANES), F32)
        sums = lax.fori_loop(0, count // rows, chunk, (zero,) * (CONV + 1))
        for j in range(CONV + 1):
            gsum_ref[j : j + 1, lanes] = jnp.sum(sums[j], axis=0, keepdims=True)

        def shift(i, _, g=g, lanes=lanes):
            row = pl.multiple_of(i * rows, rows)
            total = None
            for j in range(CONV):
                v = cw_ref[j : j + 1, lanes] * dpre_ref[g, pl.ds(row + CONV - 1 - j, rows), :]
                total = v if total is None else total + v
            din_ref[pl.ds(row, rows), lanes] = total.astype(BF)
            return 0

        lax.fori_loop(0, count // rows, shift, 0)
    gwx_ref[...] = jnp.dot(dcpt_ref[...], low_ref[...], preferred_element_type=F32)


def conv_back(inner, dx, dcpt, wxt, cw, cb, width=256):
    count, channels = inner.shape
    width = min(width, channels)
    cols = wxt.shape[0]
    return pl.pallas_call(
        conv_back_kernel,
        name="conv_back",
        grid=(channels // width,),
        in_specs=[
            pl.BlockSpec((count, width), lambda c: (0, c)),
            pl.BlockSpec((count, width), lambda c: (0, c)),
            pl.BlockSpec((count, cols), lambda c: (0, 0)),
            pl.BlockSpec((cols, count), lambda c: (0, 0)),
            pl.BlockSpec((cols, width), lambda c: (0, c)),
            pl.BlockSpec((CONV, width), lambda c: (0, c)),
            pl.BlockSpec((1, width), lambda c: (0, c)),
        ],
        out_specs=[
            pl.BlockSpec((count, width), lambda c: (0, c)),
            pl.BlockSpec((SUB, width), lambda c: (0, c)),
            pl.BlockSpec((cols, width), lambda c: (0, c)),
        ],
        out_shape=[
            jax.ShapeDtypeStruct((count, channels), BF),
            jax.ShapeDtypeStruct((SUB, channels), F32),
            jax.ShapeDtypeStruct((cols, channels), F32),
        ],
        scratch_shapes=[
            pltpu.VMEM((width // LANES, count + SUB, LANES), F32),
            pltpu.VMEM((width // LANES, count + SUB, LANES), F32),
            pltpu.VMEM((count, width), BF),
            pltpu.VMEM((count, width), F32),
        ],
        compiler_params=pltpu.CompilerParams(vmem_limit_bytes=40 << 20),
        cost_estimate=work(15e-6),
    )(inner, dx, dcpt.T, dcpt, wxt, cw, cb.reshape(1, -1))


def dual_kernel(which_ref, a_ref, b_ref, wa_ref, wb_ref, norm_ref, out_ref, sum_ref):
    del which_ref
    nt = (((1,), (1,)), ((), ()))
    out = lax.dot_general(a_ref[...], wa_ref[...], nt, preferred_element_type=F32)
    out = out + lax.dot_general(b_ref[...], wb_ref[...], nt, preferred_element_type=F32)
    out_ref[...] = out.astype(out_ref.dtype)
    sum_ref[...] = jnp.sum(norm_ref[...].astype(F32) * out, axis=0, keepdims=True)


def dual_product(which, rows, a, b, wa, wb, norm, dtype, tile=512):
    depth, count = a.shape[1], wa.shape[0]
    left = pl.BlockSpec((rows, depth), lambda n, w: (w[0], 0))
    right = pl.BlockSpec((tile, depth), lambda n, w: (n, 0))
    return pl.pallas_call(
        dual_kernel,
        name="dual_product",
        grid_spec=pltpu.PrefetchScalarGridSpec(
            num_scalar_prefetch=1,
            grid=(count // tile,),
            in_specs=[left, left, right, right, pl.BlockSpec((rows, tile), lambda n, w: (w[0], n))],
            out_specs=[
                pl.BlockSpec((rows, tile), lambda n, w: (0, n)),
                pl.BlockSpec((1, tile), lambda n, w: (0, n)),
            ],
        ),
        out_shape=[jax.ShapeDtypeStruct((rows, count), dtype), jax.ShapeDtypeStruct((1, count), F32)],
        compiler_params=pltpu.CompilerParams(vmem_limit_bytes=40 << 20),
        cost_estimate=work(15e-6),
    )(which.reshape(1).astype(jnp.int32), a, b, wa, wb, norm)


def swap(value):
    return lax.ppermute(value, "tensor", [(0, 1), (1, 0)])


def ordered(own, other):
    first = lax.axis_index("tensor") == 0
    return jnp.concatenate([jnp.where(first, own, other), jnp.where(first, other, own)], axis=0)


def gather_rows(own):
    if lax.axis_size("tensor") != 2:
        return lax.all_gather(own, "tensor", axis=0, tiled=True)
    return ordered(own, swap(own))


def total_tensor(part):
    if lax.axis_size("tensor") != 2:
        return lax.psum(part.astype(F32), "tensor")
    return part.astype(F32) + swap(part).astype(F32)


def dp_spot():
    index = lax.axis_index("dp")
    return index // 4, (index // 2) % 2, index % 2


def over_core(v):
    return lax.ppermute(v, "dp", [(i, i ^ 1) for i in range(16)])


def over_x(v):
    return lax.ppermute(v, "dp", [(i, i ^ 2) for i in range(16)])


def over_near(v):
    return lax.ppermute(v, "dp", [(i, i ^ 4) for i in range(16)])


def over_far(v):
    return lax.ppermute(v, "dp", [(i, i ^ 8) for i in range(16)])


def over_z(v, shift):
    return lax.ppermute(v, "dp", [(i, (i + 4 * shift) % 16) for i in range(16)])


def part_of(v, which, count):
    size = v.shape[0] // count
    return lax.dynamic_slice_in_dim(v, which * size, size, 0)


def pick(v, which, axis):
    return lax.dynamic_index_in_dim(v, which, axis, keepdims=False)


def add_low(*terms):
    return sum(t.astype(F32) for t in terms).astype(BF)


def paired(own, other, place):
    first = place == 0
    return jnp.concatenate([jnp.where(first, own, other), jnp.where(first, other, own)], axis=0)


def mm(a, b):
    return jnp.dot(a, b, preferred_element_type=F32)


def mm_nt(a, b):
    return lax.dot_general(a, b, (((1,), (1,)), ((), ())), preferred_element_type=F32)


def mm_tn(a, b):
    return lax.dot_general(a, b, (((0,), (0,)), ((), ())), preferred_element_type=F32)


def rows_out(residual, branch, length, first_row):
    live = first_row + jnp.arange(residual.shape[0], dtype=jnp.int32) < length
    return (residual + jnp.where(live[:, None], branch, 0.0)).astype(BF)


def rows_back(cotangent, residual, scale, gain, d_normed):
    weighted = d_normed * gain
    return (
        cotangent[0].astype(F32)
        + scale * weighted
        - residual * (scale * scale * scale) * jnp.mean(residual * weighted, axis=1, keepdims=True)
    )


def body(
    tokens,
    lengths,
    gain,
    w_in,
    conv_weight,
    conv_bias,
    w_x,
    w_dt,
    dt_bias,
    a_log,
    d_skip,
    w_out,
    cotangent,
):
    rows_here = tokens.shape[1]
    width = conv_bias.shape[0]
    total_rows = rows_here * lax.axis_size("tensor")
    paired_tensor = lax.axis_size("tensor") == 2
    grouped_dp = lax.axis_size("dp") == 16
    length = lengths[0]
    side = lax.axis_index("tensor")
    residual = tokens[0].astype(F32)
    scale = lax.rsqrt(jnp.mean(residual * residual, axis=1, keepdims=True) + EPS)
    normed = gather_rows((residual * scale * gain).astype(BF))
    cot_own = after(cotangent[0], normed)
    cot_other = swap(cot_own) if paired_tensor else lax.all_gather(cot_own, "tensor", axis=0, tiled=True)
    w_inner = lax.all_gather(w_in[:, 0], "dp", axis=0, tiled=True)
    w_gate = lax.all_gather(w_in[:, 1], "dp", axis=0, tiled=True)
    out_full = lax.all_gather(w_out, "dp", axis=1, tiled=True)
    w_x_t = w_x.T

    inner = mm(normed, w_inner)
    conv_low, part = conv_forward(inner, w_x_t, conv_weight, conv_bias, BF)
    cot_own, cot_other, part_kept = lax.optimization_barrier((cot_own, cot_other, part))
    cot_rows = ordered(cot_own, cot_other) if paired_tensor else cot_other
    live_all = jnp.arange(total_rows, dtype=jnp.int32) < length
    d_branch = jnp.where(live_all[:, None], cot_rows, jnp.zeros_like(cot_rows))
    if paired_tensor:
        coupled = part_kept.astype(F32) + after(swap(part), d_branch).astype(F32)
    else:
        coupled = total_tensor(part)
    low_t = coupled[:RANK].astype(BF)
    scanned, step_size, slope, states, last, input_lanes, output_lanes = scan_fwd(
        low_t, w_dt, dt_bias, conv_low, coupled[RANK : RANK + STATE], coupled[RANK + STATE :], a_log
    )
    w_gate, scanned = lax.optimization_barrier((w_gate, scanned))
    gate_in = mm(normed, w_gate)
    sig = jax.nn.sigmoid(gate_in)
    opened = gate_in * sig
    mixed = scanned + d_skip * conv_low.astype(F32)
    gated = (mixed * opened).astype(BF)

    def spread(grad):
        return lax.psum_scatter(grad, "dp", scatter_dimension=0, tiled=True)

    part_out = mm_tn(d_branch, gated).astype(BF)
    g_w_out = spread(part_out)
    out_full = after(out_full, part_out)
    d_gated = mm_nt(d_branch, out_full)
    d_mixed = d_gated * opened
    d_gate = (d_gated * mixed * (sig * (1.0 + gate_in * (1.0 - sig)))).astype(BF)
    part_gate = mm_tn(normed, d_gate).astype(BF)
    g_w_gate = spread(part_gate)

    def halves(v, which):
        return lax.dynamic_slice_in_dim(v, which * rows_here, rows_here, 0)

    d_mixed = after(d_mixed, part_gate)
    if not paired_tensor:
        branch = lax.psum_scatter(mm(gated, out_full), "tensor", scatter_dimension=0, tiled=True)

    d_scan, d_part, g_w_dt, g_a_log, g_vec = scan_bwd(
        low_t,
        w_dt,
        conv_low,
        d_mixed,
        step_size,
        slope,
        states,
        last,
        input_lanes,
        output_lanes,
        a_log,
        d_skip,
    )

    def joined(blocks):
        return jnp.swapaxes(blocks, 0, 1).reshape(blocks.shape[1], width)

    def packed(pieces):
        held = sum(p.shape[0] for p in pieces)
        padded = -(-held // 64) * 64
        return jnp.concatenate([p.astype(BF) for p in pieces] + [jnp.zeros((padded - held, width), BF)], axis=0)

    if paired_tensor:
        branch_sent = mm(after(halves(gated, 1 - side), d_part), out_full).astype(BF)
        d_coupled = (d_part.astype(F32) + after(swap(d_part), branch_sent).astype(F32)).astype(BF)
        branch_got = swap(after(branch_sent, d_coupled))
    else:
        d_coupled = total_tensor(d_part).astype(BF)
    d_inner, g_conv, g_w_x = conv_back(inner, d_scan, d_coupled, w_x_t, conv_weight, conv_bias)
    smalls = [joined(g_w_dt), joined(g_a_log), joined(g_vec), g_w_x, g_conv]
    if not grouped_dp or not paired_tensor:
        smalls = lax.psum(packed(smalls), "dp").astype(F32)
        g_w_inner = spread(mm_tn(normed, d_inner).astype(BF)).astype(F32)
        d_normed = lax.psum_scatter(
            mm_nt(d_inner, w_inner) + mm_nt(d_gate, w_gate), "tensor", scatter_dimension=0, tiled=True
        )
        g_gain = lax.psum(jnp.sum(residual * scale * d_normed, axis=0), ("dp", "tensor"))
        if paired_tensor:
            branch = mm(halves(gated, side), out_full) + branch_got.astype(F32)
        d_rows = rows_back(cotangent, residual, scale, gain, d_normed)
        mixed_out = rows_out(residual, branch, length, side * rows_here)
    else:
        z, x, c = dp_spot()
        own, cut = w_in.shape[0], (7 * width) // 16

        pack = packed(smalls)
        core_got = over_core(part_of(pack, 1 - c, 2))
        part_b = mm_tn(after(normed, pack), d_inner[:, cut:]).astype(BF)
        half = add_low(part_of(pack, c, 2), after(core_got, part_b))
        x_got = over_x(part_of(half, 1 - x, 2))
        chips = after(part_b, half).reshape(8, 2, own, width - cut)
        chip_sent = pick(chips, 1 - c, 1)
        chip_got = over_core(chip_sent)
        part_a = mm_tn(after(normed, chip_sent), d_inner[:, :cut]).astype(BF)
        g_a = spread(part_a)
        quarter = add_low(part_of(half, x, 2), after(x_got, part_a))
        near_got = over_near(quarter)
        chip = add_low(pick(chips, c, 1), after(chip_got, quarter)).reshape(4, 2, own, width - cut)
        row_sent = pick(chip, 1 - x, 1)
        row_got = over_x(row_sent)
        sent, gain_sent = dual_product(
            1 - side, rows_here, after(d_inner, row_sent), d_gate, w_inner, w_gate, normed, BF
        )
        normed_got = swap(sent)
        pair = add_low(quarter, after(near_got, sent))
        far_got = over_far(pair)
        kept, gain_kept = dual_product(side, rows_here, after(d_inner, pair), d_gate, w_inner, w_gate, normed, F32)
        g_gain = gain_sent + gain_kept
        gain_got = over_core(g_gain)
        row = add_low(pick(chip, x, 1), after(row_got, kept))
        column_sent = [pick(row, (z + k) % 4, 0) for k in (1, 2, 3)]
        column_got = [over_z(column_sent[k - 1], k) for k in (1, 2, 3)]
        whole = add_low(pair, *lax.optimization_barrier((far_got,) + tuple(column_sent))[:1])
        x_got = over_x(whole)
        g_gain = g_gain + after(gain_got, whole)
        gain_got = over_x(g_gain)
        branch = mm(after(halves(gated, side), g_gain), out_full) + branch_got.astype(F32)
        mixed_out = rows_out(residual, branch, length, side * rows_here)
        half = paired(whole, after(x_got, mixed_out), x)
        core_got = over_core(half)
        g_gain = g_gain + after(gain_got, mixed_out)
        gain_got = over_near(g_gain)
        smalls = paired(half, after(core_got, g_gain), c).astype(F32)
        g_gain = g_gain + after(gain_got, smalls)
        gain_got = over_far(g_gain)
        d_normed = kept + after(normed_got, g_gain).astype(F32)
        d_rows = rows_back(cotangent, residual, scale, gain, d_normed)
        g_gain = g_gain + after(gain_got, d_rows)
        gain_got = swap(g_gain)
        g_b = sum(
            (v.astype(F32) for v in lax.optimization_barrier(tuple(column_got) + (d_rows, g_gain))[:3]),
            pick(row, z, 0).astype(F32),
        )
        g_gain = (g_gain + after(gain_got, g_b))[0] / gain
        g_w_inner = jnp.concatenate([after(g_a, g_b).astype(F32), g_b], axis=1)

    g_w_dt = smalls[:RANK]
    at = RANK + STATE
    g_a_log = smalls[RANK:at]
    g_dt_bias, g_d_skip = smalls[at], smalls[at + 1]
    at += 2
    g_w_x = smalls[at : at + RANK + 2 * STATE].T
    at += RANK + 2 * STATE
    g_conv_weight = smalls[at : at + CONV]
    g_conv_bias = smalls[at + CONV]
    g_w_gate, g_w_out = lax.optimization_barrier((g_w_gate, g_w_out, d_rows))[:2]
    g_w_in = jnp.stack([g_w_inner, g_w_gate.astype(F32)], axis=1)
    return (
        mixed_out[None],
        d_rows[None],
        g_gain,
        g_w_in,
        g_conv_weight,
        g_conv_bias,
        g_w_x,
        g_w_dt,
        g_dt_bias,
        g_a_log,
        g_d_skip,
        g_w_out.T.astype(F32),
    )


def solution(mesh):
    placed = (
        P("dp", "tensor", None),
        P("dp"),
        P(),
        P("dp", None, "tensor"),
        P(None, "tensor"),
        P("tensor"),
        P("tensor", None),
        P(None, "tensor"),
        P("tensor"),
        P(None, "tensor"),
        P("tensor"),
        P("tensor", "dp"),
        P("dp", "tensor", None),
    )
    return jax.shard_map(
        body,
        mesh=mesh,
        in_specs=placed,
        out_specs=(
            P("dp", "tensor", None),
            P("dp", "tensor", None),
            P(),
            P("dp", None, "tensor"),
            P(None, "tensor"),
            P("tensor"),
            P("tensor", None),
            P(None, "tensor"),
            P("tensor"),
            P(None, "tensor"),
            P("tensor"),
            P("tensor", "dp"),
        ),
        check_vma=False,
    )
```
